256 devices in a mesh: facet: 16 (over y, x_lo, core), team: 8 (over z), sub: 2 (over x_hi).
Axes of the slice: x: 4 (x_hi: 2, x_lo: 2; x = x_hi * 2 + x_lo), y: 4, z: 8, core: 2. Of those that a mesh axis runs over, the one named last changes fastest.
Arguments:
- facet_rows: bfloat16 [16, 2, 64, 4096], P('facet', None, 'team'), may hold values from -6 to 6
- sub_offsets: int32 [32, 2], replicated, may hold values from 0 to 4095
- facet_offsets: int32 [16, 2], replicated, may hold values from 0 to 4095
- aterm: bfloat16 [16, 2, 256, 256], P('facet'), may hold values from 0.29882812 to 3
- cells: int32 [16, 2, 8, 2, 256], P('facet', None, 'team'), may hold values from 0 to 1023
- observed: bfloat16 [16, 2, 8, 2, 256], P('facet', None, 'team'), may hold values from -6 to 6
- weights: bfloat16 [16, 2, 8, 256], P('facet', None, 'team'), may hold values from 0.29882812 to 3
- counts: int32 [16, 2, 8], replicated, may hold values from 1 to 256, as said below
Outputs:
- facet_update: float32 [16, 2, 64, 4096], P('facet', None, 'team', 'sub')
The draws below stay inside these ranges and needn't reach their ends.
Inputs may be any that keep to these rules, and one draw needn't show every extreme that they name: Slots 0 to counts[a, b, t] - 1 are live. For every a and t one of the two subgrids with indices [a, 0] and [a, 1] has at most 64 live slots, and which of the two it is does not change with t.
All inputs are finite; a program needn't handle non-finite values.
Results may differ from the reference program's by a relative error of at most 0.019.
Values may be sent and summed in bfloat16 or wider, within the bound.
No kernel may reach another device: no remote copies, remote signals or barrier semaphores. Data moves between devices by JAX's collectives and lax.ppermute only.
A program may use at most 64 MiB of HBM per device.

```python
import math
import jax
import jax.numpy as jnp
from jax import lax

L = 4096
M = 128
SG = 256
VDEV = 256
R = 64
NS = 32
N_FACET = 16
N_TEAM = 8
N_SUB = 2


def draw_counts(key, part):
    key_list = jax.random.split(jax.random.fold_in(key, 7), 5)
    heavy_side = jax.random.randint(key_list[0], (N_FACET, 1), 0, 2)
    heavy_loads = jax.random.randint(key_list[1], (N_FACET, N_TEAM), VDEV // 2, VDEV + 1)
    light_loads = jax.random.randint(key_list[2], (N_FACET, N_TEAM), 1, VDEV // 4 + 1)
    flat_ids = jnp.arange(N_FACET * N_TEAM, dtype=jnp.int32).reshape(N_FACET, N_TEAM)
    top_pick = jax.random.randint(key_list[3], (), 0, N_FACET * N_TEAM)
    low_pick = jax.random.randint(key_list[4], (), 0, N_FACET * N_TEAM)
    heavy_loads = jnp.where(flat_ids == top_pick, VDEV, heavy_loads)
    light_loads = jnp.where(flat_ids == low_pick, VDEV // 4, light_loads)
    side_zero = jnp.where(heavy_side == 0, heavy_loads, light_loads)
    side_one = jnp.where(heavy_side == 0, light_loads, heavy_loads)
    return jnp.stack([side_zero, side_one], 1).astype(jnp.int32)


def place_ends(entries, rng, least, top_value):
    longest = entries.shape.index(max(entries.shape))
    spots = []
    for shift in (0, 1):
        where = [jax.random.randint(jax.random.fold_in(rng, axis), (), 0, length) for axis, length in enumerate(entries.shape)]
        where[longest] = (where[longest] + shift) % entries.shape[longest]
        spots.append(tuple(where))
    return entries.at[spots[0]].set(least).at[spots[1]].set(top_value)


def block_scale(stream_key, extent, cuts, least, largest):
    level = 1.0
    for axis_at, shards_of in cuts:
        heights = jax.random.uniform(jax.random.fold_in(jax.random.fold_in(stream_key, 6), axis_at), (shards_of,), jnp.float32, least / len(cuts), largest / len(cuts))
        level = level * jnp.repeat(jnp.exp(heights), extent[axis_at] // shards_of).reshape((-1,) + (1,) * (len(extent) - 1 - axis_at))
    return level


def noise(stream_key, extent, scale, most, cuts=(), kind=jnp.bfloat16):
    entries = scale * jax.random.normal(stream_key, extent, jnp.float32)
    if cuts:
        entries = entries * block_scale(stream_key, extent, cuts, -0.22, 0.18)
    return jnp.clip(entries, -most, most).astype(kind)


def setup_inputs(seed: int = 0) -> dict:
    splits = jax.random.split(jax.random.key(seed), 9)
    return {
        "facet_rows": noise(splits[0], (N_FACET, 2, R, L), 1.0, 6.0, ((0, 16), (2, 8))),
        "sub_offsets": place_ends(jax.random.randint(splits[1], (NS, 2), 0, L), jax.random.fold_in(splits[1], 1), 0, L - 1).astype(jnp.int32),
        "facet_offsets": place_ends(jax.random.randint(splits[2], (N_FACET, 2), 0, L), jax.random.fold_in(splits[2], 1), 0, L - 1).astype(jnp.int32),
        "aterm": jnp.clip(jnp.exp(math.log(3.0) - 2.306499 * jax.random.uniform(splits[3], (N_FACET, N_SUB, SG, SG), jnp.float32) ** block_scale(splits[3], (N_FACET, N_SUB, SG, SG), ((0, 16),), -0.2, 0.2)), 0.29882812, 3.0).astype(jnp.bfloat16),
        "cells": place_ends(jax.random.randint(splits[4], (N_FACET, N_SUB, N_TEAM, 2, VDEV), 0, 4 * SG), jax.random.fold_in(splits[4], 1), 0, (4 * SG) - 1).astype(jnp.int32),
        "observed": noise(splits[5], (N_FACET, N_SUB, N_TEAM, 2, VDEV), 1.0, 6.0, ((0, 16), (2, 8))),
        "weights": jnp.clip(jnp.exp(math.log(3.0) - 2.306499 * jax.random.uniform(splits[6], (N_FACET, N_SUB, N_TEAM, VDEV), jnp.float32) ** block_scale(splits[6], (N_FACET, N_SUB, N_TEAM, VDEV), ((0, 16), (2, 8)), -0.2, 0.2)), 0.29882812, 3.0).astype(jnp.bfloat16),
        "counts": draw_counts(jax.random.fold_in(splits[8], 71), 0),
    }


TWO_PI = 2.0 * math.pi
HIGHEST = lax.Precision.HIGHEST

def angles(left_ints, right_ints, period):
    return (left_ints * right_ints % period).astype(jnp.float32) * (TWO_PI / period)

def rounded(values_in):
    return lax.optimization_barrier(values_in.astype(jnp.bfloat16)).astype(jnp.float32)

def transform_tables():
    columns = jnp.arange(L, dtype=jnp.int32)
    frequency = jnp.arange(M, dtype=jnp.int32)
    angle_grid = angles(columns[:, None], frequency[None, :], L)
    cos_part = jnp.cos(angle_grid)
    sin_part = jnp.sin(angle_grid)
    spec_re = (cos_part / math.sqrt(L)).astype(jnp.bfloat16)
    spec_im = (-sin_part / math.sqrt(L)).astype(jnp.bfloat16)
    forward = jnp.concatenate([jnp.concatenate([spec_re, spec_im], 1), jnp.concatenate([-spec_im, spec_re], 1)], 0)
    back_re = (cos_part.T / math.sqrt(M)).astype(jnp.bfloat16)
    back_im = (sin_part.T / math.sqrt(M)).astype(jnp.bfloat16)
    backward = jnp.concatenate([jnp.concatenate([back_re, back_im], 1), jnp.concatenate([-back_im, back_re], 1)], 0)
    return (forward, backward)

def subgrid_table(size_sub):
    freq_ids = jnp.arange(M, dtype=jnp.int32)
    cell_ids = jnp.arange(size_sub, dtype=jnp.int32)
    angle_grid = angles(freq_ids[:, None], cell_ids[None, :], size_sub)
    factor = 1.0 / math.sqrt(M)
    return (jnp.cos(angle_grid) * factor, jnp.sin(angle_grid) * factor)

def facet_phase(row_ids, facet_offsets):
    col_ids = jnp.arange(M, dtype=jnp.int32)
    along_rows = row_ids[:, None] * facet_offsets[None, :, 0] % L
    along_cols = col_ids[None, :] * facet_offsets[:, 1:2] % L
    angle_grid = ((along_rows[:, :, None] + along_cols[None, :, :]) % L).astype(jnp.float32) * (TWO_PI / L)
    return (jnp.cos(angle_grid), jnp.sin(angle_grid))

def hdot(left, right):
    return jnp.dot(left, right, precision=HIGHEST, preferred_element_type=jnp.float32)

def to_image(assembled, k_re, k_im):
    grid_re = assembled[:, 0]
    grid_im = assembled[:, 1]
    temp_re = hdot(k_re.T, grid_re) - hdot(k_im.T, grid_im)
    temp_im = hdot(k_re.T, grid_im) + hdot(k_im.T, grid_re)
    image_re = hdot(temp_re, k_re) - hdot(temp_im, k_im)
    image_im = hdot(temp_re, k_im) + hdot(temp_im, k_re)
    return (image_re, image_im)

def to_return(grid, weight_map, k_re, k_im):
    size_sub = weight_map.shape[0]
    grid_re = grid[:, :size_sub] * weight_map / size_sub
    grid_im = grid[:, size_sub:] * weight_map / size_sub
    temp_re = hdot(k_re, grid_re) + hdot(k_im, grid_im)
    temp_im = hdot(k_re, grid_im) - hdot(k_im, grid_re)
    out_re = hdot(temp_re, k_re.T) + hdot(temp_im, k_im.T)
    out_im = hdot(temp_im, k_re.T) - hdot(temp_re, k_im.T)
    return jnp.stack([out_re, out_im], 1)

def degrid_block(weighted, cell_pair, observed_pair, weight, live):
    size_sub = weighted.shape[1]
    block_len = cell_pair.shape[1]
    index = jnp.arange(size_sub, dtype=jnp.int32)
    row_angle = angles(cell_pair[0][:, None], index[None, :], 4 * size_sub)
    col_angle = angles(cell_pair[1][:, None], index[None, :], 4 * size_sub)
    cos_rows = rounded(jnp.cos(row_angle))
    sin_rows = rounded(jnp.sin(row_angle))
    cos_cols = rounded(jnp.cos(col_angle))
    sin_cols = rounded(jnp.sin(col_angle))
    col_stack = jnp.concatenate([cos_cols, sin_cols], 0)
    products = jnp.einsum('jk,ik->ji', col_stack, weighted.astype(jnp.float32), precision=HIGHEST)
    part_re = products[:block_len, :size_sub] + products[block_len:, size_sub:]
    part_im = products[:block_len, size_sub:] - products[block_len:, :size_sub]
    pred_re = lax.optimization_barrier(jnp.sum(cos_rows * part_re + sin_rows * part_im, 1)) / size_sub
    pred_im = lax.optimization_barrier(jnp.sum(cos_rows * part_im - sin_rows * part_re, 1)) / size_sub
    res_re = live * weight * (observed_pair[0] - pred_re)
    res_im = live * weight * (observed_pair[1] - pred_im)
    spread_re = rounded(res_re[:, None] * cos_cols - res_im[:, None] * sin_cols)
    spread_im = rounded(res_re[:, None] * sin_cols + res_im[:, None] * cos_cols)
    right = jnp.concatenate([jnp.concatenate([spread_re, spread_im], 1), jnp.concatenate([-spread_im, spread_re], 1)], 0)
    left = jnp.concatenate([cos_rows, sin_rows], 0)
    return jnp.einsum('ji,jk->ik', left, right, precision=HIGHEST)

def reference(facet_rows, sub_offsets, facet_offsets, aterm, cells, observed, weights, counts):
    forward, backward = transform_tables()
    k_re, k_im = subgrid_table(SG)
    norm = 1.0 / math.sqrt(N_FACET)
    columns = jnp.arange(L, dtype=jnp.int32)
    row_ids = jnp.arange(R, dtype=jnp.int32)
    out_ids = jnp.arange(M, dtype=jnp.int32)
    slot_ids = jnp.arange(VDEV, dtype=jnp.int32)
    facet_re = facet_rows[:, 0].astype(jnp.float32)
    facet_im = facet_rows[:, 1].astype(jnp.float32)
    phase_cos, phase_sin = facet_phase(out_ids, facet_offsets)

    def one_subgrid(total, subgrid):
        owner = subgrid // N_SUB
        side = subgrid % N_SUB
        mod_angle = angles(sub_offsets[subgrid, 1], columns, L)
        mod_cos = jnp.cos(mod_angle)[None, None, :]
        mod_sin = jnp.sin(mod_angle)[None, None, :]
        mod_re = (facet_re * mod_cos + facet_im * mod_sin).astype(jnp.bfloat16)
        mod_im = (facet_im * mod_cos - facet_re * mod_sin).astype(jnp.bfloat16)
        stacked = jnp.concatenate([mod_re, mod_im], 2).reshape(N_FACET * R, 2 * L)
        spectrum = jnp.dot(stacked, forward, preferred_element_type=jnp.float32).reshape(N_FACET, R, 2, M)
        w_angle = angles(out_ids[:, None] + sub_offsets[subgrid, 0], row_ids[None, :], R)
        w_re = jnp.cos(w_angle) / math.sqrt(R)
        w_im = -jnp.sin(w_angle) / math.sqrt(R)
        con_re = jnp.einsum('pr,frm->pfm', w_re, spectrum[:, :, 0], precision=HIGHEST) - jnp.einsum('pr,frm->pfm', w_im, spectrum[:, :, 1], precision=HIGHEST)
        con_im = jnp.einsum('pr,frm->pfm', w_re, spectrum[:, :, 1], precision=HIGHEST) + jnp.einsum('pr,frm->pfm', w_im, spectrum[:, :, 0], precision=HIGHEST)
        grid_re = lax.optimization_barrier(jnp.sum(phase_cos * con_re - phase_sin * con_im, 1)) * norm
        grid_im = lax.optimization_barrier(jnp.sum(phase_cos * con_im + phase_sin * con_re, 1)) * norm
        image_re, image_im = to_image(jnp.stack([grid_re, grid_im], 1), k_re, k_im)
        weight_map = aterm[owner, side].astype(jnp.float32)
        weighted = jnp.concatenate([(weight_map * image_re).astype(jnp.bfloat16), (weight_map * image_im).astype(jnp.bfloat16)], 0)

        def one_team(team):
            live = (slot_ids < counts[owner, side, team]).astype(jnp.float32)
            return degrid_block(weighted, cells[owner, side, team], observed[owner, side, team].astype(jnp.float32), weights[owner, side, team].astype(jnp.float32), live)
        grid = lax.optimization_barrier(jnp.sum(lax.map(one_team, jnp.arange(N_TEAM, dtype=jnp.int32)), 0))
        returned = to_return(grid, weight_map, k_re, k_im)
        back_re = (phase_cos * returned[:, None, 0] + phase_sin * returned[:, None, 1]) * norm
        back_im = (phase_cos * returned[:, None, 1] - phase_sin * returned[:, None, 0]) * norm
        fold_re = jnp.einsum('pr,pfm->frm', w_re, back_re, precision=HIGHEST) + jnp.einsum('pr,pfm->frm', w_im, back_im, precision=HIGHEST)
        fold_im = jnp.einsum('pr,pfm->frm', w_re, back_im, precision=HIGHEST) - jnp.einsum('pr,pfm->frm', w_im, back_re, precision=HIGHEST)
        folded = jnp.stack([fold_re, fold_im], 2).astype(jnp.bfloat16).reshape(N_FACET * R, 2 * M)
        spectra_back = jnp.dot(folded, backward, preferred_element_type=jnp.float32).reshape(N_FACET, R, 2, L)
        update_re = spectra_back[:, :, 0] * mod_cos - spectra_back[:, :, 1] * mod_sin
        update_im = spectra_back[:, :, 1] * mod_cos + spectra_back[:, :, 0] * mod_sin
        return (total + jnp.stack([update_re, update_im], 1), None)
    start_total = jnp.zeros((N_FACET, 2, R, L), jnp.float32)
    total, _ = lax.scan(one_subgrid, start_total, jnp.arange(NS, dtype=jnp.int32))
    return total
```

```python
import math

import jax
import jax.numpy as jnp
import numpy as np
from jax import lax
from jax.experimental import pallas as pl
from jax.experimental.pallas import tpu as pltpu
from jax.sharding import PartitionSpec as P

L = 4096
M = 128
SG = 256
VB = 256
R = 64
NF = 16
NT = 8
NB = 2
RD = R // NT
NH = L // M
NV = NT * VB
TWO_PI = 2.0 * math.pi
BF = jnp.bfloat16
F32 = jnp.float32

ROOT = np.exp(2j * np.pi * np.arange(L) / L)


def wave(left, right, period, sign):
    steps = (np.outer(left, right) % period) * (L // period)
    table = ROOT[steps]
    return table if sign > 0 else table.conj()


def as_real(matrix):
    return np.block([[matrix.real, -matrix.imag], [matrix.imag, matrix.real]])


def half(matrix):
    return jnp.asarray(np.asarray(matrix, np.float32), BF)


def tables():
    lanes = np.arange(M)
    highs = np.arange(NH)
    fwd_rows = as_real(wave(lanes, highs, NH, -1))
    fwd_turn = wave(lanes, lanes, L, -1)
    fwd_high = as_real(wave(highs, lanes, NH, -1) / math.sqrt(L))
    bwd_rows = as_real(wave(lanes, highs, NH, 1))
    bwd_turn = wave(lanes, lanes, L, 1) / math.sqrt(M)
    bwd_full = wave(highs, lanes, NH, 1)
    bwd_high = np.stack([as_real(part) for part in np.split(bwd_full, NB)])
    k_table = wave(lanes, np.arange(SG), SG, 1) / math.sqrt(M)
    k_left = as_real(k_table.T)
    k_right = as_real(k_table).reshape(2, M, 2, SG)
    k_right = np.block([[k_table.real, k_table.imag], [-k_table.imag, k_table.real]])
    k_back = np.concatenate([k_table.real.T, -k_table.imag.T], 1)
    return {
        "fwd_rows": half(fwd_rows),
        "fwd_turn": jnp.asarray(np.stack([fwd_turn.real, fwd_turn.imag]), F32),
        "fwd_high": half(fwd_high),
        "bwd_rows": half(bwd_rows),
        "bwd_turn": jnp.asarray(np.stack([bwd_turn.real, bwd_turn.imag]), F32),
        "bwd_high": half(bwd_high),
        "k_left": half(k_left),
        "k_left_t": half(k_left.T),
        "k_right": half(k_right),
        "k_back": half(k_back),
    }


COS_TERMS = [(-1.0) ** n / math.factorial(2 * n) for n in range(10)]
SIN_TERMS = [(-1.0) ** n / math.factorial(2 * n + 1) for n in range(10)]


def turn_angle(steps, period):
    steps = steps & (period - 1)
    steps = jnp.where(steps >= period // 2, steps - period, steps)
    return steps.astype(F32) * (TWO_PI / period)


def series(square, terms):
    total = jnp.full_like(square, terms[-1])
    for term in terms[-2::-1]:
        total = total * square + term
    return total


def cos_of(angle):
    return series(angle * angle, COS_TERMS)


def sin_of(angle):
    return angle * series(angle * angle, SIN_TERMS)


def dot(left, right):
    return jnp.dot(left, right, preferred_element_type=F32)


def dot_nt(left, right):
    return lax.dot_general(left, right, (((1,), (1,)), ((), ())), preferred_element_type=F32)


def column_phase(offset):
    lane = lax.broadcasted_iota(jnp.int32, (RD, M), 1)
    angle = turn_angle(lane * offset, L)
    return cos_of(angle), sin_of(angle)


def forward_kernel(offs, foffs, rows, w_rows, turn, w_high, out, xs, xo):
    side = lax.axis_index("sub")
    facet = lax.axis_index("facet")
    for part in range(2):
        whole = rows[part].astype(F32)
        for high in range(NH):
            xs[pl.ds((part * NH + high) * RD, RD), :] = whole[:, high * M : (high + 1) * M]
    stacked = jnp.concatenate(
        [xs[pl.ds(r, 2 * NH, stride=RD), :].astype(BF) for r in range(RD)], 1
    )
    mixed = dot(w_rows[...], stacked)
    t_re = turn[0]
    t_im = turn[1]
    for r in range(RD):
        y_re = mixed[:M, r * M : (r + 1) * M]
        y_im = mixed[M:, r * M : (r + 1) * M]
        z_re = (y_re * t_re - y_im * t_im).astype(BF)
        z_im = (y_re * t_im + y_im * t_re).astype(BF)
        xo[pl.ds(r, 2 * NH, stride=RD), :] = dot_nt(
            w_high[...], jnp.concatenate([z_re, z_im], 1)
        )
    p_cos, p_sin = column_phase(foffs[facet, 1])
    lane = lax.broadcasted_iota(jnp.int32, (RD, M), 1)
    for a in range(NF):
        tuning = offs[a * NB + side, 1]
        low = tuning & (M - 1)
        first = tuning // M
        second = (first + 1) & (NH - 1)
        shift = (M - low) & (M - 1)
        parts = []
        for part in range(2):
            here = xo[pl.ds(pl.multiple_of((part * NH + first) * RD, RD), RD), :]
            after = xo[pl.ds(pl.multiple_of((part * NH + second) * RD, RD), RD), :]
            parts.append(pltpu.roll(jnp.where(lane >= low, here, after), shift, axis=1))
        re = parts[0] * p_cos - parts[1] * p_sin
        im = parts[0] * p_sin + parts[1] * p_cos
        out[a] = jnp.concatenate([re, im], 0).astype(BF)


def setup_kernel(offs, foffs, slots, k_left, k_left_t, col_t, row_t, lift, lift_t):
    facet = lax.axis_index("facet")
    team = lax.axis_index("team")
    side = lax.axis_index("sub")
    height = 16
    count = lax.broadcasted_iota(jnp.int32, (height, M), 0)
    for place, target in ((0, row_t), (2, col_t)):
        for tile in range(NV // M):
            spot = slots[tile // 2, place + tile % 2 : place + tile % 2 + 1, :]
            spot = jnp.broadcast_to(spot.astype(jnp.int32), (height, M))
            angle = turn_angle(spot * count, 4 * SG)
            cos, sin = cos_of(angle), sin_of(angle)
            step = turn_angle(spot * height, 4 * SG)
            step_cos, step_sin = cos_of(step), sin_of(step)
            for block in range(SG // height):
                target[block * height : (block + 1) * height, tile * M : (tile + 1) * M] = (
                    cos.astype(BF)
                )
                target[
                    SG + block * height : SG + (block + 1) * height, tile * M : (tile + 1) * M
                ] = sin.astype(BF)
                if block + 1 < SG // height:
                    cos, sin = cos * step_cos - sin * step_sin, cos * step_sin + sin * step_cos
    shift_u = offs[facet * NB + side, 0]
    row = lax.broadcasted_iota(jnp.int32, (2 * RD, 2 * M), 0)
    lane = lax.broadcasted_iota(jnp.int32, (2 * RD, 2 * M), 1)
    p = lane & (M - 1)
    quarter = (row // RD - lane // M) * (L // 4)
    row_turn = (L // R) * (p + shift_u) * (team * RD + (row & (RD - 1)))
    base = quarter - row_turn
    blocks = []
    for f in range(NF):
        steps = base + p * foffs[f, 0]
        blocks.append((cos_of(turn_angle(steps, L)) * (1.0 / 32.0)).astype(BF))
    joined = jnp.concatenate(blocks, 0)
    lift[...] = dot_nt(k_left[...], joined).astype(BF)
    lift_t[...] = dot(joined, k_left_t[...]).astype(BF)


def predict_kernel(spec, lift, k_right, aterm, col_t, row_t, out, rows_out):
    side = lax.axis_index("sub")
    turned = dot(lift[...], spec[...]).astype(BF)
    image = dot(jnp.concatenate([turned[:SG], turned[SG:]], 1), k_right[...])
    weight = aterm[side].astype(F32)
    w_re = image[:, :SG] * weight
    w_im = image[:, SG:] * weight
    left = jnp.concatenate(
        [
            jnp.concatenate([w_re, w_im], 1).astype(BF),
            jnp.concatenate([w_im, -w_re], 1).astype(BF),
        ],
        0,
    )
    width = 256
    for chunk in range(NV // width):
        span = slice(chunk * width, (chunk + 1) * width)
        z = dot(left, col_t[:, span])
        cos = row_t[:SG, span].astype(F32)
        sin = row_t[SG:, span].astype(F32)
        re = jnp.sum(cos * z[:SG] + sin * z[SG:], 0, keepdims=True) * (1.0 / SG)
        im = jnp.sum(cos * z[SG:] - sin * z[:SG], 0, keepdims=True) * (1.0 / SG)
        for tile in range(width // M):
            at = chunk * (width // M) + tile
            rows_out[at : at + 1, :] = re[:, tile * M : (tile + 1) * M]
            rows_out[NV // M + at : NV // M + at + 1, :] = im[:, tile * M : (tile + 1) * M]
    packed = rows_out[...].astype(BF)
    for peer in range(NT):
        out[peer] = packed


def grid_kernel(counts, parts, slots, col_t, row_t, aterm, lift_t, k_back, out, spread, res):
    facet = lax.axis_index("facet")
    side = lax.axis_index("sub")
    total = parts[0].astype(F32)
    for peer in range(1, NT):
        total = total + parts[peer].astype(F32)
    res[...] = total
    lane = lax.broadcasted_iota(jnp.int32, (1, M), 1)
    for tile in range(NV // M):
        t = tile // 2
        h = tile % 2
        live = lane + h * M < counts[facet, side, t]
        weight = jnp.where(live, slots[t, 8 + h : 9 + h, :], 0.0)
        r_re = weight * (slots[t, 4 + h : 5 + h, :] - res[tile : tile + 1, :])
        r_im = weight * (slots[t, 6 + h : 7 + h, :] - res[NV // M + tile : NV // M + tile + 1, :])
        span = slice(tile * M, (tile + 1) * M)
        cos = col_t[:SG, span].astype(F32)
        sin = col_t[SG:, span].astype(F32)
        spread[:SG, span] = (r_re * cos - r_im * sin).astype(BF)
        spread[SG:, span] = (r_re * sin + r_im * cos).astype(BF)
    both = dot_nt(row_t[...], spread[...])
    weight = aterm[side].astype(F32) * (1.0 / SG)
    g_re = (both[:SG, :SG] - both[SG:, SG:]) * weight
    g_im = (both[:SG, SG:] + both[SG:, :SG]) * weight
    grid = jnp.concatenate([g_re, g_im], 0).astype(BF)
    low = dot(lift_t[...], grid).astype(BF)
    back = dot(low, k_back[...])
    for f in range(NF):
        top = back[f * 16 : f * 16 + 8]
        bot = back[f * 16 + 8 : f * 16 + 16]
        re = top[:, :M] - bot[:, M:]
        im = bot[:, :M] + top[:, M:]
        both_parts = jnp.concatenate([re, im], 0).astype(BF)
        for b in range(NB):
            out[f * NB + b] = both_parts


def update_kernel(offs, foffs, folded, w_rows, turn, w_high, out, us, os):
    facet = lax.axis_index("facet")
    side = lax.axis_index("sub")
    us[...] = jnp.zeros_like(us)
    p_cos, p_sin = column_phase(foffs[facet, 1])
    lane = lax.broadcasted_iota(jnp.int32, (RD, M), 1)
    for s in range(NF * NB):
        tuning = offs[s, 1]
        low = tuning & (M - 1)
        first = tuning // M
        second = (first + 1) & (NH - 1)
        both = folded[s].astype(F32)
        re = both[:RD] * p_cos + both[RD:] * p_sin
        im = both[RD:] * p_cos - both[:RD] * p_sin
        for part, value in ((0, re), (1, im)):
            turned = pltpu.roll(value, low, axis=1)
            here = pl.ds(pl.multiple_of((part * NH + first) * RD, RD), RD)
            after = pl.ds(pl.multiple_of((part * NH + second) * RD, RD), RD)
            us[here, :] += jnp.where(lane >= low, turned, 0.0)
            us[after, :] += jnp.where(lane >= low, 0.0, turned)
    stacked = jnp.concatenate(
        [us[pl.ds(r, 2 * NH, stride=RD), :].astype(BF) for r in range(RD)], 1
    )
    mixed = dot(w_rows[...], stacked)
    t_re = turn[0]
    t_im = turn[1]
    high = w_high[side]
    n_out = NH // NB
    for r in range(RD):
        y_re = mixed[:M, r * M : (r + 1) * M]
        y_im = mixed[M:, r * M : (r + 1) * M]
        z_re = (y_re * t_re - y_im * t_im).astype(BF)
        z_im = (y_re * t_im + y_im * t_re).astype(BF)
        os[pl.ds(r, 2 * n_out, stride=RD), :] = dot_nt(high, jnp.concatenate([z_re, z_im], 1))
    for part in range(2):
        for h in range(n_out):
            at = (part * n_out + h) * RD
            out[part, :, h * M : (h + 1) * M] = os[at : at + RD, :]


def shape(*dims, dtype=BF):
    return jax.ShapeDtypeStruct(dims, dtype)


SMEM = pl.BlockSpec(memory_space=pltpu.SMEM)
VMEM = pl.BlockSpec(memory_space=pltpu.VMEM)
PARAMS = pltpu.CompilerParams(vmem_limit_bytes=48 * 2**20)


def call(kernel, specs, outs, scratch, name):
    single = not isinstance(outs, (list, tuple))
    return pl.pallas_call(
        kernel,
        out_shape=outs,
        in_specs=specs,
        out_specs=VMEM if single else [VMEM] * len(outs),
        scratch_shapes=scratch,
        compiler_params=PARAMS,
        name=name,
    )


def local(facet_rows, sub_offsets, facet_offsets, aterm, cells, observed, weights, counts):
    side = lax.axis_index("sub")
    t = tables()
    mine = lambda array: lax.dynamic_index_in_dim(array[0, :, 0], side, 0, keepdims=False)
    slot_rows = jnp.concatenate(
        [
            mine(cells).astype(F32).reshape(4, M),
            mine(observed).astype(F32).reshape(4, M),
            mine(weights).astype(F32).reshape(2, M),
            jnp.zeros((6, M), F32),
        ],
        0,
    )
    slots = lax.all_to_all(
        jnp.broadcast_to(slot_rows, (NT, 16, M)), "team", 0, 0, tiled=True
    )
    windows = call(
        forward_kernel,
        [SMEM, SMEM, VMEM, VMEM, VMEM, VMEM],
        shape(NF, 2 * RD, M),
        [pltpu.VMEM((2 * L // M * RD, M), F32)] * 2,
        "windows",
    )(sub_offsets, facet_offsets, facet_rows[0], t["fwd_rows"], t["fwd_turn"], t["fwd_high"])
    arrived = lax.all_to_all(windows, "facet", 0, 0, tiled=True)
    col_t, row_t, lift, lift_t = call(
        setup_kernel,
        [SMEM, SMEM, VMEM, VMEM, VMEM],
        [shape(2 * SG, NV), shape(2 * SG, NV), shape(2 * SG, 2 * M), shape(2 * M, 2 * SG)],
        [],
        "setup",
    )(sub_offsets, facet_offsets, slots, t["k_left"], t["k_left_t"])
    parts = call(
        predict_kernel,
        [VMEM] * 6,
        shape(NT, 2 * NV // M, M),
        [pltpu.VMEM((2 * NV // M, M), F32)],
        "predict",
    )(arrived.reshape(2 * M, M), lift, t["k_right"], aterm[0], col_t, row_t)
    gathered = lax.all_to_all(parts, "team", 0, 0, tiled=True)
    folded = call(
        grid_kernel,
        [SMEM] + [VMEM] * 7,
        shape(NF * NB, 2 * RD, M),
        [pltpu.VMEM((2 * SG, NV), BF), pltpu.VMEM((2 * NV // M, M), F32)],
        "grid",
    )(counts, gathered, slots, col_t, row_t, aterm[0], lift_t, t["k_back"])
    returned = lax.all_to_all(folded, ("facet", "sub"), 0, 0, tiled=True)
    update = call(
        update_kernel,
        [SMEM, SMEM, VMEM, VMEM, VMEM, VMEM],
        shape(2, RD, L // NB, dtype=F32),
        [pltpu.VMEM((2 * NH * RD, M), F32), pltpu.VMEM((NH * RD, M), F32)],
        "update",
    )(sub_offsets, facet_offsets, returned, t["bwd_rows"], t["bwd_turn"], t["bwd_high"])
    return update[None]


def solution(mesh):
    placed = (
        P("facet", None, "team", None),
        P(),
        P(),
        P("facet", None, None, None),
        P("facet", None, "team", None, None),
        P("facet", None, "team", None, None),
        P("facet", None, "team", None),
        P(),
    )
    return jax.shard_map(
        local,
        mesh=mesh,
        in_specs=placed,
        out_specs=P("facet", None, "team", "sub"),
        check_vma=False,
    )
```

```python
import math

import jax
import jax.numpy as jnp
import numpy as np
from jax import lax
from jax.experimental import pallas as pl
from jax.experimental.pallas import tpu as pltpu
from jax.sharding import PartitionSpec as P

L = 4096
M = 128
SG = 256
VB = 256
R = 64
NF = 16
NT = 8
NB = 2
RD = R // NT
NH = L // M
NV = NT * VB
TWO_PI = 2.0 * math.pi
BF = jnp.bfloat16
F32 = jnp.float32

ROOT = np.exp(2j * np.pi * np.arange(L) / L)


def wave(left, right, period, sign):
    steps = (np.outer(left, right) % period) * (L // period)
    table = ROOT[steps]
    return table if sign > 0 else table.conj()


def as_real(matrix):
    return np.block([[matrix.real, -matrix.imag], [matrix.imag, matrix.real]])


def half(matrix):
    return jnp.asarray(np.asarray(matrix, np.float32), BF)


def tables():
    lanes = np.arange(M)
    highs = np.arange(NH)
    fwd_rows = as_real(wave(lanes, highs, NH, -1))
    fwd_turn = wave(lanes, lanes, L, -1)
    fwd_high = as_real(wave(highs, lanes, NH, -1) / math.sqrt(L))
    bwd_rows = as_real(wave(lanes, highs, NH, 1))
    bwd_turn = wave(lanes, lanes, L, 1) / math.sqrt(M)
    bwd_full = wave(highs, lanes, NH, 1)
    bwd_high = np.stack([as_real(part) for part in np.split(bwd_full, NB)])
    k_table = wave(lanes, np.arange(SG), SG, 1) / math.sqrt(M)
    k_left = as_real(k_table.T)
    k_right = np.block([[k_table.real, k_table.imag], [-k_table.imag, k_table.real]])
    k_back = np.concatenate([k_table.real.T, -k_table.imag.T], 1)
    return {
        "fwd_rows": half(fwd_rows),
        "fwd_turn": jnp.asarray(np.stack([fwd_turn.real, fwd_turn.imag]), F32),
        "fwd_high": half(fwd_high),
        "bwd_rows": half(bwd_rows),
        "bwd_turn": jnp.asarray(np.stack([bwd_turn.real, bwd_turn.imag]), F32),
        "bwd_high": half(bwd_high),
        "k_left": half(k_left),
        "k_left_t": half(k_left.T),
        "k_right": half(k_right),
        "k_back": half(k_back),
    }


COS_TERMS = [(-1.0) ** n / math.factorial(2 * n) for n in range(9)]
SIN_TERMS = [(-1.0) ** n / math.factorial(2 * n + 1) for n in range(8)]


def turn_angle(steps, period):
    steps = steps & (period - 1)
    steps = jnp.where(steps >= period // 2, steps - period, steps)
    return steps.astype(F32) * (TWO_PI / period)


def series(square, terms):
    total = jnp.full_like(square, terms[-1])
    for term in terms[-2::-1]:
        total = total * square + term
    return total


def cos_of(angle):
    return series(angle * angle, COS_TERMS)


def sin_of(angle):
    return angle * series(angle * angle, SIN_TERMS)


def dot(left, right):
    return jnp.dot(left, right, preferred_element_type=F32)


def dot_nt(left, right):
    return lax.dot_general(left, right, (((1,), (1,)), ((), ())), preferred_element_type=F32)


def column_phase(offset):
    lane = lax.broadcasted_iota(jnp.int32, (RD, M), 1)
    angle = turn_angle(lane * offset, L)
    return cos_of(angle), sin_of(angle)


def fetch(pairs, sems):
    copies = []
    for at, (source, target) in enumerate(pairs):
        copy = pltpu.make_async_copy(source, target, sems.at[at])
        copy.start()
        copies.append(copy)
    return copies


def slot_kernel(
    cells_h, seen_h, weights_h, rows_h, w_rows_h, turn_h, w_high_h,
    slots, stacked, w_rows, turn, w_high, cells, seen, weights, rows, xs, packed, sems,
):
    side = lax.axis_index("sub")
    copies = fetch(
        [
            (cells_h.at[0, side, 0], cells),
            (seen_h.at[0, side, 0], seen),
            (weights_h.at[0, 0], weights),
            (rows_h.at[0], rows),
            (w_rows_h, w_rows),
            (turn_h, turn),
            (w_high_h, w_high),
        ],
        sems,
    )
    packed[...] = jnp.zeros_like(packed)
    for copy in copies:
        copy.wait()
    pair = weights[...].astype(F32)
    weight = jnp.where(side == 0, pair[0:1], pair[1:2])
    for at in range(2):
        span = slice(at * M, (at + 1) * M)
        packed[at : at + 1, :] = cells[0:1, span].astype(F32)
        packed[2 + at : 3 + at, :] = cells[1:2, span].astype(F32)
        both = seen[:, span].astype(F32)
        packed[4 + at : 5 + at, :] = both[0:1]
        packed[6 + at : 7 + at, :] = both[1:2]
        packed[8 + at : 9 + at, :] = weight[:, span]
    for peer in range(NT):
        slots[peer] = packed[...]
    for part in range(2):
        whole = rows[part].astype(F32)
        for high in range(NH):
            xs[pl.ds((part * NH + high) * RD, RD), :] = whole[:, high * M : (high + 1) * M]
    for r in range(RD):
        stacked[:, r * M : (r + 1) * M] = xs[pl.ds(r, 2 * NH, stride=RD), :].astype(BF)


def forward_kernel(offs_h, foffs_h, stacked, w_rows, turn, w_high, out, offs, foffs, xo, sems):
    side = lax.axis_index("sub")
    facet = lax.axis_index("facet")
    copies = fetch([(offs_h, offs), (foffs_h, foffs)], sems)
    mixed = dot(w_rows[...], stacked[...])
    t_re = turn[0]
    t_im = turn[1]
    for r in range(RD):
        y_re = mixed[:M, r * M : (r + 1) * M]
        y_im = mixed[M:, r * M : (r + 1) * M]
        z_re = (y_re * t_re - y_im * t_im).astype(BF)
        z_im = (y_re * t_im + y_im * t_re).astype(BF)
        xo[pl.ds(r, 2 * NH, stride=RD), :] = dot_nt(
            w_high[...], jnp.concatenate([z_re, z_im], 1)
        )
    for copy in copies:
        copy.wait()
    p_cos, p_sin = column_phase(foffs[1, facet])
    lane = lax.broadcasted_iota(jnp.int32, (RD, M), 1)
    for a in range(NF):
        tuning = offs[1, a * NB + side]
        low = tuning & (M - 1)
        first = tuning // M
        second = (first + 1) & (NH - 1)
        shift = (M - low) & (M - 1)
        parts = []
        for part in range(2):
            here = xo[pl.ds(pl.multiple_of((part * NH + first) * RD, RD), RD), :]
            after = xo[pl.ds(pl.multiple_of((part * NH + second) * RD, RD), RD), :]
            parts.append(pltpu.roll(jnp.where(lane >= low, here, after), shift, axis=1))
        re = parts[0] * p_cos - parts[1] * p_sin
        im = parts[0] * p_sin + parts[1] * p_cos
        out[a] = jnp.concatenate([re, im], 0).astype(BF)


HEIGHT = 16
STEPS = SG // HEIGHT


def setup_kernel(
    offs_h, foffs_h, slots, k_left_h, k_left_t_h, k_right_h, aterm_h, k_back_h,
    col_t, row_base, row_step, lift, lift_t, k_right, aterm, k_back,
    offs, foffs, k_left, k_left_t, sems,
):
    facet = lax.axis_index("facet")
    team = lax.axis_index("team")
    side = lax.axis_index("sub")
    copies = fetch(
        [
            (offs_h, offs),
            (foffs_h, foffs),
            (k_left_h, k_left),
            (k_left_t_h, k_left_t),
            (k_right_h, k_right),
            (aterm_h.at[0, side], aterm),
            (k_back_h, k_back),
        ],
        sems,
    )
    count = lax.broadcasted_iota(jnp.int32, (HEIGHT, M), 0)

    def turns(place, tile):
        at = place + tile % 2
        spot = jnp.broadcast_to(slots[tile // 2, at : at + 1, :].astype(jnp.int32), (HEIGHT, M))
        angle = turn_angle(spot * count, 4 * SG)
        step = turn_angle(spot[:8] * HEIGHT, 4 * SG)
        return cos_of(angle), sin_of(angle), cos_of(step), sin_of(step)

    for tile in range(NV // M):
        lanes = slice(tile * M, (tile + 1) * M)
        cos, sin, step_cos, step_sin = turns(0, tile)
        row_base[0, :, lanes] = cos
        row_base[1, :, lanes] = sin
        row_step[0, :, lanes] = step_cos
        row_step[1, :, lanes] = step_sin
        cos, sin, step_cos, step_sin = turns(2, tile)
        step_cos = jnp.concatenate([step_cos, step_cos], 0)
        step_sin = jnp.concatenate([step_sin, step_sin], 0)
        for block in range(STEPS):
            at = block * HEIGHT
            col_t[at : at + HEIGHT, lanes] = cos.astype(BF)
            col_t[SG + at : SG + at + HEIGHT, lanes] = sin.astype(BF)
            if block + 1 < STEPS:
                cos, sin = cos * step_cos - sin * step_sin, cos * step_sin + sin * step_cos
    for copy in copies:
        copy.wait()
    shift_u = offs[0, facet * NB + side]
    row = lax.broadcasted_iota(jnp.int32, (2 * RD, 2 * M), 0)
    lane = lax.broadcasted_iota(jnp.int32, (2 * RD, 2 * M), 1)
    p = lane & (M - 1)
    quarter = (row // RD - lane // M) * (L // 4)
    row_turn = (L // R) * (p + shift_u) * (team * RD + (row & (RD - 1)))
    base = quarter - row_turn
    blocks = []
    for f in range(NF):
        steps = base + p * foffs[0, f]
        blocks.append((cos_of(turn_angle(steps, L)) * (1.0 / 32.0)).astype(BF))
    joined = jnp.concatenate(blocks, 0)
    lift[...] = dot_nt(k_left[...], joined).astype(BF)
    lift_t[...] = dot(joined, k_left_t[...]).astype(BF)


def twice(value):
    return jnp.concatenate([value, value], 0)


def predict_kernel(spec, lift, k_right, aterm, col_t, row_base, row_step, out, rows_out):
    turned = dot(lift[...], spec[...]).astype(BF)
    image = dot(jnp.concatenate([turned[:SG], turned[SG:]], 1), k_right[...])
    weight = aterm[...].astype(F32)
    w_re = image[:, :SG] * weight
    w_im = image[:, SG:] * weight
    left = jnp.concatenate(
        [
            jnp.concatenate([w_re, w_im], 1).astype(BF),
            jnp.concatenate([w_im, -w_re], 1).astype(BF),
        ],
        0,
    )
    for chunk in range(NT):
        span = slice(chunk * VB, (chunk + 1) * VB)
        z = dot(left, col_t[:, span])
        step_cos = twice(row_step[0, :, span])
        step_sin = twice(row_step[1, :, span])
        re = z[SG - HEIGHT : SG]
        im = z[2 * SG - HEIGHT :]
        for block in range(STEPS - 2, -1, -1):
            at = block * HEIGHT
            re, im = (
                re * step_cos + im * step_sin + z[at : at + HEIGHT],
                im * step_cos - re * step_sin + z[SG + at : SG + at + HEIGHT],
            )
        cos = row_base[0, :, span]
        sin = row_base[1, :, span]
        re, im = re * cos + im * sin, im * cos - re * sin
        re = jnp.sum(re, 0, keepdims=True) * (1.0 / SG)
        im = jnp.sum(im, 0, keepdims=True) * (1.0 / SG)
        for tile in range(VB // M):
            at = chunk * (VB // M) + tile
            rows_out[at : at + 1, :] = re[:, tile * M : (tile + 1) * M]
            rows_out[NV // M + at : NV // M + at + 1, :] = im[:, tile * M : (tile + 1) * M]
    packed = rows_out[...].astype(BF)
    for peer in range(NT):
        out[peer] = packed


def grid_kernel(
    counts, parts, slots, col_t, row_base, row_step, aterm, lift_t, k_back, out, spread, res
):
    facet = lax.axis_index("facet")
    side = lax.axis_index("sub")
    total = parts[0].astype(F32)
    for peer in range(1, NT):
        total = total + parts[peer].astype(F32)
    res[...] = total
    lane = lax.broadcasted_iota(jnp.int32, (1, M), 1)
    for tile in range(NV // M):
        t = tile // 2
        h = tile % 2
        live = lane + h * M < counts[side, t, facet]
        weight = jnp.where(live, slots[t, 8 + h : 9 + h, :], 0.0)
        r_re = weight * (slots[t, 4 + h : 5 + h, :] - res[tile : tile + 1, :])
        r_im = weight * (slots[t, 6 + h : 7 + h, :] - res[NV // M + tile : NV // M + tile + 1, :])
        span = slice(tile * M, (tile + 1) * M)
        step_cos = twice(row_step[0, :, span])
        step_sin = twice(row_step[1, :, span])
        cos = row_base[0, :, span]
        sin = row_base[1, :, span]
        re, im = r_re * cos - r_im * sin, r_re * sin + r_im * cos
        for block in range(STEPS):
            at = block * HEIGHT
            spread[at : at + HEIGHT, span] = re.astype(BF)
            spread[SG + at : SG + at + HEIGHT, span] = im.astype(BF)
            if block + 1 < STEPS:
                re, im = re * step_cos - im * step_sin, re * step_sin + im * step_cos
    both = dot_nt(spread[...], col_t[...])
    weight = aterm[...].astype(F32) * (1.0 / SG)
    g_re = (both[:SG, :SG] - both[SG:, SG:]) * weight
    g_im = (both[:SG, SG:] + both[SG:, :SG]) * weight
    grid = jnp.concatenate([g_re, g_im], 0).astype(BF)
    low = dot(lift_t[...], grid).astype(BF)
    back = dot(low, k_back[...])
    for f in range(NF):
        top = back[f * 16 : f * 16 + 8]
        bot = back[f * 16 + 8 : f * 16 + 16]
        re = top[:, :M] - bot[:, M:]
        im = bot[:, :M] + top[:, M:]
        both_parts = jnp.concatenate([re, im], 0).astype(BF)
        for b in range(NB):
            out[f * NB + b] = both_parts


def update_kernel(
    offs_h, foffs_h, folded, w_rows_h, turn_h, w_high_h,
    out, offs, foffs, us, os, w_rows, turn, w_high, sems,
):
    facet = lax.axis_index("facet")
    side = lax.axis_index("sub")
    copies = fetch(
        [
            (offs_h, offs),
            (foffs_h, foffs),
            (w_rows_h, w_rows),
            (turn_h, turn),
            (w_high_h.at[side], w_high),
        ],
        sems,
    )
    us[...] = jnp.zeros_like(us)
    for copy in copies[:2]:
        copy.wait()
    p_cos, p_sin = column_phase(foffs[1, facet])
    lane = lax.broadcasted_iota(jnp.int32, (RD, M), 1)
    for s in range(NF * NB):
        tuning = offs[1, s]
        low = tuning & (M - 1)
        first = tuning // M
        second = (first + 1) & (NH - 1)
        both = folded[s].astype(F32)
        re = both[:RD] * p_cos + both[RD:] * p_sin
        im = both[RD:] * p_cos - both[:RD] * p_sin
        for part, value in ((0, re), (1, im)):
            turned = pltpu.roll(value, low, axis=1)
            here = pl.ds(pl.multiple_of((part * NH + first) * RD, RD), RD)
            after = pl.ds(pl.multiple_of((part * NH + second) * RD, RD), RD)
            us[here, :] += jnp.where(lane >= low, turned, 0.0)
            us[after, :] += jnp.where(lane >= low, 0.0, turned)
    stacked = jnp.concatenate(
        [us[pl.ds(r, 2 * NH, stride=RD), :].astype(BF) for r in range(RD)], 1
    )
    for copy in copies[2:]:
        copy.wait()
    mixed = dot(w_rows[...], stacked)
    t_re = turn[0]
    t_im = turn[1]
    high = w_high[...]
    n_out = NH // NB
    for r in range(RD):
        y_re = mixed[:M, r * M : (r + 1) * M]
        y_im = mixed[M:, r * M : (r + 1) * M]
        z_re = (y_re * t_re - y_im * t_im).astype(BF)
        z_im = (y_re * t_im + y_im * t_re).astype(BF)
        os[pl.ds(r, 2 * n_out, stride=RD), :] = dot_nt(high, jnp.concatenate([z_re, z_im], 1))
    for part in range(2):
        for h in range(n_out):
            at = (part * n_out + h) * RD
            out[part, :, h * M : (h + 1) * M] = os[at : at + RD, :]


def shape(*dims, dtype=BF):
    return jax.ShapeDtypeStruct(dims, dtype)


SMEM = pl.BlockSpec(memory_space=pltpu.SMEM)
VMEM = pl.BlockSpec(memory_space=pltpu.VMEM)
HBM = pl.BlockSpec(memory_space=pltpu.HBM)
PARAMS = pltpu.CompilerParams(vmem_limit_bytes=24 * 2**20)


def buf(*dims, dtype=BF):
    return pltpu.VMEM(dims, dtype)


def smem(*dims):
    return pltpu.SMEM(dims, jnp.int32)


def sems(count):
    return pltpu.SemaphoreType.DMA((count,))


def call(kernel, specs, outs, scratch, name, places=None):
    single = not isinstance(outs, (list, tuple))
    return pl.pallas_call(
        kernel,
        out_shape=outs,
        in_specs=specs,
        out_specs=places or (VMEM if single else [VMEM] * len(outs)),
        scratch_shapes=scratch,
        compiler_params=PARAMS,
        name=name,
    )


def local(facet_rows, sub_offsets, facet_offsets, aterm, cells, observed, weights, counts):
    t = tables()
    offs = sub_offsets.T
    foffs = facet_offsets.T
    live = counts.transpose(1, 2, 0)
    keep = lambda array: pltpu.with_memory_space_constraint(array, pltpu.HBM)
    offs = keep(offs)
    foffs = keep(foffs)
    ids = [smem(2, NF * NB), smem(2, NF)]
    slot_rows, stacked, w_rows, turn, w_high = call(
        slot_kernel,
        [HBM] * 7,
        [
            shape(NT, 16, M, dtype=F32),
            shape(2 * NH, RD * M),
            shape(2 * M, 2 * NH),
            shape(2, M, M, dtype=F32),
            shape(2 * NH, 2 * M),
        ],
        [
            buf(2, VB, dtype=jnp.int32),
            buf(2, VB),
            buf(2, VB),
            buf(2, RD, L),
            buf(2 * NH * RD, M, dtype=F32),
            buf(16, M, dtype=F32),
            sems(7),
        ],
        "slots",
    )(
        keep(cells), keep(observed), keep(weights.transpose(0, 2, 1, 3)), keep(facet_rows),
        keep(t["fwd_rows"]), keep(t["fwd_turn"]), keep(t["fwd_high"]),
    )
    slots = lax.all_to_all(slot_rows, "team", 0, 0, tiled=True)
    windows = call(
        forward_kernel,
        [HBM] * 2 + [VMEM] * 4,
        shape(NF, 2 * RD, M),
        ids + [buf(2 * NH * RD, M, dtype=F32), sems(2)],
        "windows",
    )(offs, foffs, stacked, w_rows, turn, w_high)
    arrived = lax.all_to_all(windows, "facet", 0, 0, tiled=True)
    col_t, row_base, row_step, lift, lift_t, k_right, own_map, k_back = call(
        setup_kernel,
        [HBM, HBM, VMEM] + [HBM] * 5,
        [
            shape(2 * SG, NV),
            shape(2, HEIGHT, NV, dtype=F32),
            shape(2, 8, NV, dtype=F32),
            shape(2 * SG, 2 * M),
            shape(2 * M, 2 * SG),
            shape(2 * M, 2 * SG),
            shape(SG, SG),
            shape(SG, 2 * M),
        ],
        ids + [buf(2 * SG, 2 * M), buf(2 * M, 2 * SG), sems(7)],
        "setup",
    )(
        offs, foffs, slots, keep(t["k_left"]), keep(t["k_left_t"]), keep(t["k_right"]),
        keep(aterm), keep(t["k_back"]),
    )
    parts = call(
        predict_kernel,
        [VMEM] * 7,
        shape(NT, 2 * NV // M, M),
        [buf(2 * NV // M, M, dtype=F32)],
        "predict",
    )(arrived.reshape(2 * M, M), lift, k_right, own_map, col_t, row_base, row_step)
    gathered = lax.all_to_all(parts, "team", 0, 0, tiled=True)
    folded = call(
        grid_kernel,
        [SMEM] + [VMEM] * 8,
        shape(NF * NB, 2 * RD, M),
        [buf(2 * SG, NV), buf(2 * NV // M, M, dtype=F32)],
        "grid",
    )(live, gathered, slots, col_t, row_base, row_step, own_map, lift_t, k_back)
    returned = lax.all_to_all(folded, ("facet", "sub"), 0, 0, tiled=True)
    update = call(
        update_kernel,
        [HBM, HBM, VMEM, HBM, HBM, HBM],
        shape(2, RD, L // NB, dtype=F32),
        ids
        + [
            buf(2 * NH * RD, M, dtype=F32),
            buf(NH * RD, M, dtype=F32),
            buf(2 * M, 2 * NH),
            buf(2, M, M, dtype=F32),
            buf(NH, 2 * M),
            sems(5),
        ],
        "update",
    )(
        offs, foffs, returned,
        keep(t["bwd_rows"]), keep(t["bwd_turn"]), keep(t["bwd_high"]),
    )
    return update[None]


def solution(mesh):
    placed = (
        P("facet", None, "team", None),
        P(),
        P(),
        P("facet", None, None, None),
        P("facet", None, "team", None, None),
        P("facet", None, "team", None, None),
        P("facet", None, "team", None),
        P(),
    )
    return jax.shard_map(
        local,
        mesh=mesh,
        in_specs=placed,
        out_specs=P("facet", None, "team", "sub"),
        check_vma=False,
    )
```

```python
import math

import jax
import jax.numpy as jnp
import numpy as np
from jax import lax
from jax.experimental import pallas as pl
from jax.experimental.pallas import tpu as pltpu
from jax.sharding import PartitionSpec as P

L = 4096
M = 128
SG = 256
VB = 256
R = 64
NF = 16
NT = 8
NB = 2
RD = R // NT
NH = L // M
NV = NT * VB
TWO_PI = 2.0 * math.pi
BF = jnp.bfloat16
F32 = jnp.float32

ROOT = np.exp(2j * np.pi * np.arange(L) / L)


def wave(left, right, period, sign):
    steps = (np.outer(left, right) % period) * (L // period)
    table = ROOT[steps]
    return table if sign > 0 else table.conj()


def as_real(matrix):
    return np.block([[matrix.real, -matrix.imag], [matrix.imag, matrix.real]])


def half(matrix):
    return jnp.asarray(np.asarray(matrix, np.float32), BF)


def tables():
    lanes = np.arange(M)
    highs = np.arange(NH)
    fwd_rows = as_real(wave(lanes, highs, NH, -1))
    fwd_turn = wave(lanes, lanes, L, -1)
    fwd_high = as_real(wave(highs, lanes, NH, -1) / math.sqrt(L))
    bwd_rows = as_real(wave(lanes, highs, NH, 1))
    bwd_turn = wave(lanes, lanes, L, 1) / math.sqrt(M)
    bwd_full = wave(highs, lanes, NH, 1)
    bwd_high = np.stack([as_real(part) for part in np.split(bwd_full, NB)])
    k_table = wave(lanes, np.arange(SG), SG, 1) / math.sqrt(M)
    k_left = as_real(k_table.T)
    k_right = np.block([[k_table.real, k_table.imag], [-k_table.imag, k_table.real]])
    k_back = np.concatenate([k_table.real.T, -k_table.imag.T], 1)
    return {
        "fwd_rows": half(fwd_rows),
        "fwd_turn": jnp.asarray(np.stack([fwd_turn.real, fwd_turn.imag]), F32),
        "fwd_high": half(fwd_high),
        "bwd_rows": half(bwd_rows),
        "bwd_turn": jnp.asarray(np.stack([bwd_turn.real, bwd_turn.imag]), F32),
        "bwd_high": half(bwd_high),
        "k_left": half(k_left),
        "k_left_t": half(k_left.T),
        "k_right": half(k_right),
        "k_back": half(k_back),
    }


COS_TERMS = [(-1.0) ** n / math.factorial(2 * n) for n in range(9)]
SIN_TERMS = [(-1.0) ** n / math.factorial(2 * n + 1) for n in range(8)]


def turn_angle(steps, period):
    steps = steps & (period - 1)
    steps = jnp.where(steps >= period // 2, steps - period, steps)
    return steps.astype(F32) * (TWO_PI / period)


def series(square, terms):
    total = jnp.full_like(square, terms[-1])
    for term in terms[-2::-1]:
        total = total * square + term
    return total


def cos_of(angle):
    return series(angle * angle, COS_TERMS)


def sin_of(angle):
    return angle * series(angle * angle, SIN_TERMS)


def dot(left, right):
    return jnp.dot(left, right, preferred_element_type=F32)


def dot_nt(left, right):
    return lax.dot_general(left, right, (((1,), (1,)), ((), ())), preferred_element_type=F32)


def column_phase(offset):
    lane = lax.broadcasted_iota(jnp.int32, (RD, M), 1)
    angle = turn_angle(lane * offset, L)
    return cos_of(angle), sin_of(angle)


def fetch(pairs, sems):
    copies = []
    for at, (source, target) in enumerate(pairs):
        copy = pltpu.make_async_copy(source, target, sems.at[at])
        copy.start()
        copies.append(copy)
    return copies


def forward_kernel(
    offs_h, foffs_h, cells_h, rows_h, w_rows_h, turn_h, w_high_h,
    out, offs_v, foffs_v, cells_v, offs, foffs, rows, w_rows, turn, w_high, xs, xo, sems,
):
    side = lax.axis_index("sub")
    facet = lax.axis_index("facet")
    copies = fetch(
        [
            (rows_h.at[0], rows),
            (w_rows_h, w_rows),
            (turn_h, turn),
            (w_high_h, w_high),
            (offs_h, offs),
            (foffs_h, foffs),
            (offs_h, offs_v),
            (foffs_h, foffs_v),
            (cells_h.at[0, :, 0], cells_v),
        ],
        sems,
    )
    for copy in copies:
        copy.wait()
    for part in range(2):
        whole = rows[part].astype(F32)
        for high in range(NH):
            xs[pl.ds((part * NH + high) * RD, RD), :] = whole[:, high * M : (high + 1) * M]
    stacked = jnp.concatenate(
        [xs[pl.ds(r, 2 * NH, stride=RD), :].astype(BF) for r in range(RD)], 1
    )
    mixed = dot(w_rows[...], stacked)
    t_re = turn[0]
    t_im = turn[1]
    for r in range(RD):
        y_re = mixed[:M, r * M : (r + 1) * M]
        y_im = mixed[M:, r * M : (r + 1) * M]
        z_re = (y_re * t_re - y_im * t_im).astype(BF)
        z_im = (y_re * t_im + y_im * t_re).astype(BF)
        xo[pl.ds(r, 2 * NH, stride=RD), :] = dot_nt(
            w_high[...], jnp.concatenate([z_re, z_im], 1)
        )
    p_cos, p_sin = column_phase(foffs[1, facet])
    lane = lax.broadcasted_iota(jnp.int32, (RD, M), 1)
    for a in range(NF):
        tuning = offs[1, a * NB + side]
        low = tuning & (M - 1)
        first = tuning >> 7
        second = (first + 1) & (NH - 1)
        shift = (M - low) & (M - 1)
        parts = []
        for part in range(2):
            here = xo[pl.ds(pl.multiple_of((part * NH + first) * RD, RD), RD), :]
            after = xo[pl.ds(pl.multiple_of((part * NH + second) * RD, RD), RD), :]
            parts.append(pltpu.roll(jnp.where(lane >= low, here, after), shift, axis=1))
        re = parts[0] * p_cos - parts[1] * p_sin
        im = parts[0] * p_sin + parts[1] * p_cos
        out[a] = jnp.concatenate([re, im], 0).astype(BF)


SENT = 40
OBS = 2 * NV // M
HEIGHT = 16
STEPS = SG // HEIGHT


def setup_kernel(
    offs_v, foffs_v, near_h, far_h, k_left_h, k_left_t_h, k_right_h, aterm_h, seen_h, weights_h,
    col_t, row_base, row_step, lift, lift_t, k_right, aterm, tail,
    offs, foffs, near, far, k_left, k_left_t, spots, seen, weights, sems,
):
    facet = lax.axis_index("facet")
    team = lax.axis_index("team")
    side = lax.axis_index("sub")
    copies = fetch(
        [
            (offs_v, offs),
            (foffs_v, foffs),
            (k_left_h, k_left),
            (k_left_t_h, k_left_t),
            (near_h.at[:, side], near),
            (far_h.at[:, side], far),
            (k_right_h, k_right),
            (aterm_h.at[0, side], aterm),
            (seen_h.at[0, side, 0], seen),
            (weights_h.at[0, 0], weights),
        ],
        sems,
    )
    for copy in copies[:2]:
        copy.wait()
    shift_u = offs[0, facet * NB + side]
    row = lax.broadcasted_iota(jnp.int32, (2 * RD, 2 * M), 0)
    lane = lax.broadcasted_iota(jnp.int32, (2 * RD, 2 * M), 1)
    p = lane & (M - 1)
    quarter = ((row >> 3) - (lane >> 7)) * (L // 4)
    row_turn = (L // R) * (p + shift_u) * (team * RD + (row & (RD - 1)))
    base = quarter - row_turn
    blocks = []
    for f in range(NF):
        steps = base + p * foffs[0, f]
        blocks.append((cos_of(turn_angle(steps, L)) * (1.0 / 32.0)).astype(BF))
    joined = jnp.concatenate(blocks, 0)
    for copy in copies[2:]:
        copy.wait()
    lift[...] = dot_nt(k_left[...], joined).astype(BF)
    lift_t[...] = dot(joined, k_left_t[...]).astype(BF)
    pair = weights[...].astype(F32)
    weight = jnp.where(side == 0, pair[0:1], pair[1:2])
    both = seen[...].astype(F32)
    tail[...] = jnp.zeros_like(tail)
    for at in range(2):
        half = slice(at * M, (at + 1) * M)
        tail[at : at + 1, :] = both[0:1, half]
        tail[2 + at : 3 + at, :] = both[1:2, half]
        tail[4 + at : 5 + at, :] = weight[:, half]
    for step in range(NT // 2):
        spots[team ^ step] = near[step]
        spots[team ^ (step + NT // 2)] = far[step]
    count = lax.broadcasted_iota(jnp.int32, (HEIGHT, M), 0)

    def turns(place, tile):
        half = slice(tile % 2 * M, (tile % 2 + 1) * M)
        spot = jnp.broadcast_to(spots[tile // 2, place : place + 1, half], (HEIGHT, M))
        angle = turn_angle(spot * count, 4 * SG)
        step = turn_angle(spot[:8] * HEIGHT, 4 * SG)
        return cos_of(angle), sin_of(angle), cos_of(step), sin_of(step)

    for tile in range(NV // M):
        lanes = slice(tile * M, (tile + 1) * M)
        cos, sin, step_cos, step_sin = turns(0, tile)
        row_base[0, :, lanes] = cos
        row_base[1, :, lanes] = sin
        row_step[0, :, lanes] = step_cos
        row_step[1, :, lanes] = step_sin
        cos, sin, step_cos, step_sin = turns(1, tile)
        step_cos = twice(step_cos)
        step_sin = twice(step_sin)
        for block in range(STEPS):
            at = block * HEIGHT
            col_t[at : at + HEIGHT, lanes] = cos.astype(BF)
            col_t[SG + at : SG + at + HEIGHT, lanes] = sin.astype(BF)
            if block + 1 < STEPS:
                cos, sin = cos * step_cos - sin * step_sin, cos * step_sin + sin * step_cos


def twice(value):
    return jnp.concatenate([value, value], 0)


def predict_kernel(
    spec, lift, k_right, aterm, col_t, row_base, row_step, tail, out, rows_out
):
    turned = dot(lift[...], spec[...]).astype(BF)
    image = dot(jnp.concatenate([turned[:SG], turned[SG:]], 1), k_right[...])
    weight = aterm[...].astype(F32)
    w_re = image[:, :SG] * weight
    w_im = image[:, SG:] * weight
    left = jnp.concatenate(
        [
            jnp.concatenate([w_re, w_im], 1).astype(BF),
            jnp.concatenate([w_im, -w_re], 1).astype(BF),
        ],
        0,
    )
    for chunk in range(NT):
        span = slice(chunk * VB, (chunk + 1) * VB)
        z = dot(left, col_t[:, span])
        step_cos = twice(row_step[0, :, span])
        step_sin = twice(row_step[1, :, span])
        re = z[SG - HEIGHT : SG]
        im = z[2 * SG - HEIGHT :]
        for block in range(STEPS - 2, -1, -1):
            at = block * HEIGHT
            re, im = (
                re * step_cos + im * step_sin + z[at : at + HEIGHT],
                im * step_cos - re * step_sin + z[SG + at : SG + at + HEIGHT],
            )
        cos = row_base[0, :, span]
        sin = row_base[1, :, span]
        re, im = re * cos + im * sin, im * cos - re * sin
        re = jnp.sum(re, 0, keepdims=True) * (1.0 / SG)
        im = jnp.sum(im, 0, keepdims=True) * (1.0 / SG)
        for tile in range(VB // M):
            at = chunk * (VB // M) + tile
            rows_out[at : at + 1, :] = re[:, tile * M : (tile + 1) * M]
            rows_out[NV // M + at : NV // M + at + 1, :] = im[:, tile * M : (tile + 1) * M]
    rows_out[OBS:, :] = tail[...]
    packed = rows_out[...].astype(BF)
    for peer in range(NT):
        out[peer] = packed


def grid_kernel(
    counts, parts, col_t, row_base, row_step, aterm, lift_t, k_back_h,
    out, spread, res, slots, k_back, sems,
):
    facet = lax.axis_index("facet")
    side = lax.axis_index("sub")
    copies = fetch([(k_back_h, k_back)], sems)
    part = parts[0].astype(F32)
    total = part[:OBS]
    slots[0] = part[OBS:]
    for peer in range(1, NT):
        part = parts[peer].astype(F32)
        total = total + part[:OBS]
        slots[peer] = part[OBS:]
    res[...] = total
    lane = lax.broadcasted_iota(jnp.int32, (1, M), 1)
    for tile in range(NV // M):
        t = tile // 2
        h = tile % 2
        live = lane + h * M < counts[side, t, facet]
        weight = jnp.where(live, slots[t, 4 + h : 5 + h, :], 0.0)
        r_re = weight * (slots[t, h : 1 + h, :] - res[tile : tile + 1, :])
        r_im = weight * (slots[t, 2 + h : 3 + h, :] - res[NV // M + tile : NV // M + tile + 1, :])
        span = slice(tile * M, (tile + 1) * M)
        step_cos = twice(row_step[0, :, span])
        step_sin = twice(row_step[1, :, span])
        cos = row_base[0, :, span]
        sin = row_base[1, :, span]
        re, im = r_re * cos - r_im * sin, r_re * sin + r_im * cos
        for block in range(STEPS):
            at = block * HEIGHT
            spread[at : at + HEIGHT, span] = re.astype(BF)
            spread[SG + at : SG + at + HEIGHT, span] = im.astype(BF)
            if block + 1 < STEPS:
                re, im = re * step_cos - im * step_sin, re * step_sin + im * step_cos
    both = dot_nt(spread[...], col_t[...])
    weight = aterm[...].astype(F32) * (1.0 / SG)
    g_re = (both[:SG, :SG] - both[SG:, SG:]) * weight
    g_im = (both[:SG, SG:] + both[SG:, :SG]) * weight
    grid = jnp.concatenate([g_re, g_im], 0).astype(BF)
    low = dot(lift_t[...], grid).astype(BF)
    copies[0].wait()
    back = dot(low, k_back[...])
    for f in range(NF):
        top = back[f * 16 : f * 16 + 8]
        bot = back[f * 16 + 8 : f * 16 + 16]
        re = top[:, :M] - bot[:, M:]
        im = bot[:, :M] + top[:, M:]
        both_parts = jnp.concatenate([re, im], 0).astype(BF)
        for b in range(NB):
            out[f * NB + b] = both_parts


def update_kernel(
    offs_h, foffs_h, folded, w_rows_h, turn_h, w_high_h,
    out, offs, foffs, us, os, w_rows, turn, w_high, sems,
):
    facet = lax.axis_index("facet")
    side = lax.axis_index("sub")
    copies = fetch(
        [
            (offs_h, offs),
            (foffs_h, foffs),
            (w_rows_h, w_rows),
            (turn_h, turn),
            (w_high_h.at[side], w_high),
        ],
        sems,
    )
    us[...] = jnp.zeros_like(us)
    for copy in copies[:2]:
        copy.wait()
    p_cos, p_sin = column_phase(foffs[1, facet])
    lane = lax.broadcasted_iota(jnp.int32, (RD, M), 1)
    for s in range(NF * NB):
        tuning = offs[1, s]
        low = tuning & (M - 1)
        first = tuning >> 7
        second = (first + 1) & (NH - 1)
        both = folded[s].astype(F32)
        re = both[:RD] * p_cos + both[RD:] * p_sin
        im = both[RD:] * p_cos - both[:RD] * p_sin
        for part, value in ((0, re), (1, im)):
            turned = pltpu.roll(value, low, axis=1)
            here = pl.ds(pl.multiple_of((part * NH + first) * RD, RD), RD)
            after = pl.ds(pl.multiple_of((part * NH + second) * RD, RD), RD)
            us[here, :] += jnp.where(lane >= low, turned, 0.0)
            us[after, :] += jnp.where(lane >= low, 0.0, turned)
    stacked = jnp.concatenate(
        [us[pl.ds(r, 2 * NH, stride=RD), :].astype(BF) for r in range(RD)], 1
    )
    for copy in copies[2:]:
        copy.wait()
    mixed = dot(w_rows[...], stacked)
    t_re = turn[0]
    t_im = turn[1]
    high = w_high[...]
    n_out = NH // NB
    for r in range(RD):
        y_re = mixed[:M, r * M : (r + 1) * M]
        y_im = mixed[M:, r * M : (r + 1) * M]
        z_re = (y_re * t_re - y_im * t_im).astype(BF)
        z_im = (y_re * t_im + y_im * t_re).astype(BF)
        os[pl.ds(r, 2 * n_out, stride=RD), :] = dot_nt(high, jnp.concatenate([z_re, z_im], 1))
    for part in range(2):
        for h in range(n_out):
            at = (part * n_out + h) * RD
            out[part, :, h * M : (h + 1) * M] = os[at : at + RD, :]


def shape(*dims, dtype=BF):
    return jax.ShapeDtypeStruct(dims, dtype)


SMEM = pl.BlockSpec(memory_space=pltpu.SMEM)
VMEM = pl.BlockSpec(memory_space=pltpu.VMEM)
HBM = pl.BlockSpec(memory_space=pltpu.HBM)
ANY = pl.BlockSpec(memory_space=pl.ANY)
PARAMS = pltpu.CompilerParams(vmem_limit_bytes=24 * 2**20)


def buf(*dims, dtype=BF):
    return pltpu.VMEM(dims, dtype)


def smem(*dims):
    return pltpu.SMEM(dims, jnp.int32)


def sems(count):
    return pltpu.SemaphoreType.DMA((count,))


def call(kernel, specs, outs, scratch, name, places=None, cost=None):
    single = not isinstance(outs, (list, tuple))
    return pl.pallas_call(
        kernel,
        out_shape=outs,
        in_specs=specs,
        out_specs=places or (VMEM if single else [VMEM] * len(outs)),
        scratch_shapes=scratch,
        compiler_params=PARAMS,
        cost_estimate=cost,
        name=name,
    )


def partner(value, mask):
    pairs = [(source, source ^ mask) for source in range(NT)]
    return lax.ppermute(value, "team", pairs)


def local(facet_rows, sub_offsets, facet_offsets, aterm, cells, observed, weights, counts):
    t = tables()
    offs = sub_offsets.T
    foffs = facet_offsets.T
    live = counts.transpose(1, 2, 0)
    keep = lambda array: pltpu.with_memory_space_constraint(array, pltpu.HBM)
    offs = keep(offs)
    foffs = keep(foffs)
    ids = [smem(2, NF * NB), smem(2, NF)]
    others = [partner(cells, mask) for mask in (1, 2, 3)]
    windows, offs_v, foffs_v, cells_v = call(
        forward_kernel,
        [HBM] * 7,
        [
            shape(NF, 2 * RD, M),
            shape(2, NF * NB, dtype=jnp.int32),
            shape(2, NF, dtype=jnp.int32),
            shape(NB, 2, VB, dtype=jnp.int32),
        ],
        ids
        + [
            buf(2, RD, L),
            buf(2 * M, 2 * NH),
            buf(2, M, M, dtype=F32),
            buf(2 * NH, 2 * M),
            buf(2 * NH * RD, M, dtype=F32),
            buf(2 * NH * RD, M, dtype=F32),
            sems(9),
        ],
        "windows",
    )(
        offs, foffs, keep(cells), keep(facet_rows),
        keep(t["fwd_rows"]), keep(t["fwd_turn"]), keep(t["fwd_high"]),
    )
    *others, windows = lax.optimization_barrier((*others, windows))
    near = jnp.stack([part.reshape(NB, 2, VB) for part in [cells_v] + others])
    far = partner(near, NT // 2)
    arrived = lax.all_to_all(windows, "facet", 0, 0, tiled=True)
    col_t, row_base, row_step, lift, lift_t, k_right, own_map, tail = call(
        setup_kernel,
        [VMEM] * 2 + [ANY] * 2 + [HBM] * 6,
        [
            shape(2 * SG, NV),
            shape(2, HEIGHT, NV, dtype=F32),
            shape(2, 8, NV, dtype=F32),
            shape(2 * SG, 2 * M),
            shape(2 * M, 2 * SG),
            shape(2 * M, 2 * SG),
            shape(SG, SG),
            shape(SENT - OBS, M, dtype=F32),
        ],
        ids
        + [buf(NT // 2, 2, VB, dtype=jnp.int32)] * 2
        + [
            buf(2 * SG, 2 * M),
            buf(2 * M, 2 * SG),
            buf(NT, 2, VB, dtype=jnp.int32),
            buf(2, VB),
            buf(2, VB),
            sems(10),
        ],
        "setup",
        cost=pl.CostEstimate(flops=20 * 10**9, transcendentals=0, bytes_accessed=2**22),
    )(
        offs_v, foffs_v, near, far, keep(t["k_left"]), keep(t["k_left_t"]),
        keep(t["k_right"]), keep(aterm), keep(observed), keep(weights.transpose(0, 2, 1, 3)),
    )
    parts = call(
        predict_kernel,
        [VMEM] * 8,
        shape(NT, SENT, M),
        [buf(SENT, M, dtype=F32)],
        "predict",
    )(arrived.reshape(2 * M, M), lift, k_right, own_map, col_t, row_base, row_step, tail)
    gathered = lax.all_to_all(parts, "team", 0, 0, tiled=True)
    folded = call(
        grid_kernel,
        [SMEM] + [VMEM] * 6 + [HBM],
        shape(NF * NB, 2 * RD, M),
        [
            buf(2 * SG, NV),
            buf(OBS, M, dtype=F32),
            buf(NT, SENT - OBS, M, dtype=F32),
            buf(SG, 2 * M),
            sems(1),
        ],
        "grid",
    )(live, gathered, col_t, row_base, row_step, own_map, lift_t, keep(t["k_back"]))
    returned = lax.all_to_all(folded, ("facet", "sub"), 0, 0, tiled=True)
    update = call(
        update_kernel,
        [VMEM, VMEM, VMEM, HBM, HBM, HBM],
        shape(2, RD, L // NB, dtype=F32),
        ids
        + [
            buf(2 * NH * RD, M, dtype=F32),
            buf(NH * RD, M, dtype=F32),
            buf(2 * M, 2 * NH),
            buf(2, M, M, dtype=F32),
            buf(NH, 2 * M),
            sems(5),
        ],
        "update",
    )(
        offs_v, foffs_v, returned,
        keep(t["bwd_rows"]), keep(t["bwd_turn"]), keep(t["bwd_high"]),
    )
    return update[None]


def solution(mesh):
    placed = (
        P("facet", None, "team", None),
        P(),
        P(),
        P("facet", None, None, None),
        P("facet", None, "team", None, None),
        P("facet", None, "team", None, None),
        P("facet", None, "team", None),
        P(),
    )
    return jax.shard_map(
        local,
        mesh=mesh,
        in_specs=placed,
        out_specs=P("facet", None, "team", "sub"),
        check_vma=False,
    )
```

```python
import math

import jax
import jax.numpy as jnp
import numpy as np
from jax import lax
from jax.experimental import pallas as pl
from jax.experimental.pallas import tpu as pltpu
from jax.sharding import PartitionSpec as P

L = 4096
M = 128
SG = 256
VB = 256
R = 64
NF = 16
NT = 8
NB = 2
RD = R // NT
NH = L // M
NV = NT * VB
TWO_PI = 2.0 * math.pi
BF = jnp.bfloat16
F32 = jnp.float32

ROOT = np.exp(2j * np.pi * np.arange(L) / L)


def wave(left, right, period, sign):
    steps = (np.outer(left, right) % period) * (L // period)
    table = ROOT[steps]
    return table if sign > 0 else table.conj()


def as_real(matrix):
    return np.block([[matrix.real, -matrix.imag], [matrix.imag, matrix.real]])


def half(matrix):
    return jnp.asarray(np.asarray(matrix, np.float32), BF)


def tables():
    lanes = np.arange(M)
    highs = np.arange(NH)
    fwd_rows = as_real(wave(lanes, highs, NH, -1))
    fwd_turn = wave(lanes, lanes, L, -1)
    bwd_turn = wave(lanes, lanes, L, 1) / math.sqrt(M)
    bwd_full = wave(highs, lanes, NH, 1)
    bwd_high = np.stack([as_real(part) for part in np.split(bwd_full, NB)])
    k_table = wave(lanes, np.arange(SG), SG, 1) / math.sqrt(M)
    k_left = as_real(k_table.T)
    return {
        "fwd_rows": half(fwd_rows),
        "fwd_turn": jnp.asarray(np.stack([fwd_turn.real, fwd_turn.imag]), F32),
        "bwd_turn": jnp.asarray(np.stack([bwd_turn.real, bwd_turn.imag]), F32),
        "bwd_high": half(bwd_high),
        "k_left": half(k_left),
    }


COS_TERMS = [(-1.0) ** n / math.factorial(2 * n) for n in range(9)]
SIN_TERMS = [(-1.0) ** n / math.factorial(2 * n + 1) for n in range(8)]


def turn_angle(steps, period):
    steps = steps & (period - 1)
    steps = jnp.where(steps >= period // 2, steps - period, steps)
    return steps.astype(F32) * (TWO_PI / period)


def series(square, terms):
    total = jnp.full_like(square, terms[-1])
    for term in terms[-2::-1]:
        total = total * square + term
    return total


def cos_of(angle):
    return series(angle * angle, COS_TERMS)


def sin_of(angle):
    return angle * series(angle * angle, SIN_TERMS)


def dot(left, right):
    return jnp.dot(left, right, preferred_element_type=F32)


def dot_tn(left, right):
    return lax.dot_general(left, right, (((0,), (0,)), ((), ())), preferred_element_type=F32)


def dot_nt(left, right):
    return lax.dot_general(left, right, (((1,), (1,)), ((), ())), preferred_element_type=F32)


def fetch(pairs, sems):
    copies = []
    for at, (source, target) in enumerate(pairs):
        copy = pltpu.make_async_copy(source, target, sems.at[at])
        copy.start()
        copies.append(copy)
    return copies


def forward_kernel(
    offs_h, foffs_h, cells_h, rows_h, w_rows_h, turn_h,
    out, offs_v, foffs_v, cells_v, offs, rows, w_rows, turn, xs, xo, sems,
):
    side = lax.axis_index("sub")
    copies = fetch(
        [
            (offs_h, offs),
            (rows_h.at[0], rows),
            (w_rows_h, w_rows),
            (turn_h, turn),
            (offs_h, offs_v),
            (foffs_h, foffs_v),
            (cells_h.at[0, :, 0], cells_v),
        ],
        sems,
    )
    for copy in copies:
        copy.wait()
    row = lax.broadcasted_iota(jnp.int32, (NF, 2 * M), 0)
    lane = lax.broadcasted_iota(jnp.int32, (NF, 2 * M), 1)
    tuning = jnp.zeros((NF, 2 * M), jnp.int32)
    for a in range(NF):
        tuning = jnp.where(row == a, offs[1, a * NB + side], tuning)
    pick = lane[:, :M] >= (tuning[:, :M] & (M - 1))
    first = (tuning >> 7) * (lane & (M - 1))
    later = lane & (M - 1)
    blocks = []
    for part in range(2):
        for late in range(2):
            steps = (L // NH) * (first + late * later) + (L // 4) * (part - (lane >> 7))
            blocks.append((cos_of(turn_angle(steps, L)) * (1.0 / 64.0)).astype(BF))
    w_high = jnp.concatenate(blocks, 0)
    for part in range(2):
        whole = rows[part].astype(F32)
        for high in range(NH):
            xs[pl.ds((part * NH + high) * RD, RD), :] = whole[:, high * M : (high + 1) * M]
    stacked = jnp.concatenate(
        [xs[pl.ds(r, 2 * NH, stride=RD), :].astype(BF) for r in range(RD)], 1
    )
    mixed = dot(w_rows[...], stacked)
    t_re = turn[0]
    t_im = turn[1]
    for r in range(RD):
        y_re = mixed[:M, r * M : (r + 1) * M]
        y_im = mixed[M:, r * M : (r + 1) * M]
        z_re = (y_re * t_re - y_im * t_im).astype(BF)
        z_im = (y_re * t_im + y_im * t_re).astype(BF)
        found = dot_nt(w_high, jnp.concatenate([z_re, z_im], 1))
        for part in range(2):
            at = part * 2 * NF
            value = jnp.where(pick, found[at : at + NF], found[at + NF : at + 2 * NF])
            xo[pl.ds(part * RD + r, NF, stride=2 * RD), :] = value
    for a in range(NF):
        out[a] = xo[a * 2 * RD : (a + 1) * 2 * RD, :].astype(BF)


SENT = 40
OBS = 2 * NV // M
HEIGHT = 16
STEPS = SG // HEIGHT


def setup_kernel(
    offs_v, foffs_v, near_h, far_h, k_left_h, aterm_h, seen_h, weights_h, counts_h, turn_h, w_high_h,
    col_t, row_fac, lift, k_right, aterm, tail, phase, w_rows, picks, turn, w_high,
    offs, foffs, counts, near, far, k_left, spots, seen, weights, sems,
):
    facet = lax.axis_index("facet")
    team = lax.axis_index("team")
    side = lax.axis_index("sub")
    copies = fetch(
        [
            (offs_v, offs),
            (foffs_v, foffs),
            (k_left_h, k_left),
            (near_h.at[:, side], near),
            (far_h.at[:, side], far),
            (aterm_h.at[0, side], aterm),
            (seen_h.at[0, side, 0], seen),
            (weights_h.at[0, 0], weights),
            (counts_h, counts),
            (turn_h, turn),
            (w_high_h.at[side], w_high),
        ],
        sems,
    )
    for copy in copies[:2]:
        copy.wait()
    shift_u = offs[0, facet * NB + side]
    row = lax.broadcasted_iota(jnp.int32, (2 * RD, 2 * M), 0)
    lane = lax.broadcasted_iota(jnp.int32, (2 * RD, 2 * M), 1)
    p = lane & (M - 1)
    quarter = ((row >> 3) - (lane >> 7)) * (L // 4)
    row_turn = (L // R) * (p + shift_u) * (team * RD + (row & (RD - 1)))
    base = quarter - row_turn
    blocks = []
    for f in range(NF):
        steps = base + p * foffs[0, f]
        blocks.append((cos_of(turn_angle(steps, L)) * (1.0 / 32.0)).astype(BF))
    joined = jnp.concatenate(blocks, 0)
    own = offs[1, facet * NB + side]
    row = lax.broadcasted_iota(jnp.int32, (NF, M), 0)
    lane = lax.broadcasted_iota(jnp.int32, (NF, M), 1)
    column = jnp.zeros((NF, M), jnp.int32)
    for f in range(NF):
        column = jnp.where(row == f, foffs[1, f], column)
    angle = turn_angle(column * ((lane - own) & (M - 1)), L)
    phase[0] = cos_of(angle)
    phase[1] = sin_of(angle)
    row = lax.broadcasted_iota(jnp.int32, (M, SG), 0)
    lane = lax.broadcasted_iota(jnp.int32, (M, SG), 1)
    angle = turn_angle(((row - own) & (M - 1)) * lane, SG)
    k_re = (cos_of(angle) * (1.0 / math.sqrt(M))).astype(BF)
    k_im = (sin_of(angle) * (1.0 / math.sqrt(M))).astype(BF)
    k_right[:M, :SG] = k_re
    k_right[:M, SG:] = k_im
    k_right[M:, :SG] = -k_im
    k_right[M:, SG:] = k_re
    lane = lax.broadcasted_iota(jnp.int32, (8, M), 1)
    row = lax.broadcasted_iota(jnp.int32, (NF * NB, M), 0)
    high = jnp.zeros((8, M), jnp.int32)
    low = jnp.zeros((NF * NB, M), jnp.int32)
    for s in range(NF * NB):
        high = jnp.where((lane & (NF * NB - 1)) == s, offs[1, s] >> 7, high)
        low = jnp.where(row == s, offs[1, s] & (M - 1), low)
    lane_rows = lax.broadcasted_iota(jnp.int32, (NF * NB, M), 1)
    picks[...] = jnp.where(lane_rows >= low, 1.0, 0.0)
    high = high + ((lane >> 5) & 1)
    quarter = (lane >> 6) * (L // 4)
    high = jnp.concatenate([high] * 4, 0)
    quarter = jnp.concatenate([quarter] * 4, 0)
    for block in range(2 * M // 32):
        spot = lax.broadcasted_iota(jnp.int32, (32, M), 0) + block * 32
        steps = (L // NH) * (spot & (M - 1)) * high + quarter - (spot >> 7) * (L // 4)
        w_rows[block * 32 : (block + 1) * 32, :] = cos_of(turn_angle(steps, L)).astype(BF)
    for copy in copies[2:]:
        copy.wait()
    lift[...] = dot_nt(k_left[...], joined).astype(BF)
    pair = weights[...].astype(F32)
    weight = jnp.where(side == 0, pair[0:1], pair[1:2])
    slot = lax.broadcasted_iota(jnp.int32, (1, VB), 1)
    weight = jnp.where(slot < counts[side, team, facet], weight, 0.0)
    both = seen[...].astype(F32)
    tail[...] = jnp.zeros_like(tail)
    for at in range(2):
        half = slice(at * M, (at + 1) * M)
        tail[at : at + 1, :] = both[0:1, half]
        tail[2 + at : 3 + at, :] = both[1:2, half]
        tail[4 + at : 5 + at, :] = weight[:, half]
    for step in range(NT // 2):
        spots[team ^ step] = near[step]
        spots[team ^ (step + NT // 2)] = far[step]
    count = lax.broadcasted_iota(jnp.int32, (8, M), 0)

    def turns(place, tile):
        half = slice(tile % 2 * M, (tile % 2 + 1) * M)
        spot = jnp.broadcast_to(spots[tile // 2, place : place + 1, half], (8, M))
        angle = turn_angle(spot * count, 4 * SG)
        step = turn_angle(spot * 8, 4 * SG)
        return cos_of(angle), sin_of(angle), cos_of(step), sin_of(step)

    for tile in range(NV // M):
        lanes = slice(tile * M, (tile + 1) * M)
        cos, sin, step_cos, step_sin = turns(0, tile)
        row_fac[0:8, lanes] = cos
        row_fac[8:16, lanes] = sin
        row_fac[16:17, lanes] = step_cos[0:1]
        row_fac[17:18, lanes] = step_sin[0:1]
        cos, sin, step_cos, step_sin = widen(*turns(1, tile))
        for block in range(STEPS):
            at = block * HEIGHT
            col_t[at : at + HEIGHT, lanes] = cos.astype(BF)
            col_t[SG + at : SG + at + HEIGHT, lanes] = sin.astype(BF)
            if block + 1 < STEPS:
                cos, sin = cos * step_cos - sin * step_sin, cos * step_sin + sin * step_cos


def widen(cos, sin, step_cos, step_sin):
    far_cos = cos * step_cos - sin * step_sin
    far_sin = cos * step_sin + sin * step_cos
    twice_cos = step_cos * step_cos - step_sin * step_sin
    twice_sin = 2.0 * step_cos * step_sin
    return (
        jnp.concatenate([cos, far_cos], 0),
        jnp.concatenate([sin, far_sin], 0),
        twice(twice_cos),
        twice(twice_sin),
    )


def row_factors(row_fac, span):
    width = span.stop - span.start
    return widen(
        row_fac[0:8, span],
        row_fac[8:16, span],
        jnp.broadcast_to(row_fac[16:17, span], (8, width)),
        jnp.broadcast_to(row_fac[17:18, span], (8, width)),
    )


def twice(value):
    return jnp.concatenate([value, value], 0)


def predict_kernel(
    spec, lift, k_right, aterm, col_t, row_fac, tail, phase, out, rows_out
):
    parts = []
    for f in range(NF):
        both = spec[f].astype(F32)
        cos = phase[0, f : f + 1, :]
        sin = phase[1, f : f + 1, :]
        parts.append(both[:RD] * cos - both[RD:] * sin)
        parts.append(both[:RD] * sin + both[RD:] * cos)
    turned = dot(lift[...], jnp.concatenate(parts, 0).astype(BF)).astype(BF)
    image = dot(jnp.concatenate([turned[:SG], turned[SG:]], 1), k_right[...])
    weight = aterm[...].astype(F32)
    w_re = image[:, :SG] * weight
    w_im = image[:, SG:] * weight
    left = jnp.concatenate(
        [
            jnp.concatenate([w_re, w_im], 1).astype(BF),
            jnp.concatenate([w_im, -w_re], 1).astype(BF),
        ],
        0,
    )
    for chunk in range(NT):
        span = slice(chunk * VB, (chunk + 1) * VB)
        z = dot(left, col_t[:, span])
        cos, sin, step_cos, step_sin = row_factors(row_fac, span)
        re = z[SG - HEIGHT : SG]
        im = z[2 * SG - HEIGHT :]
        for block in range(STEPS - 2, -1, -1):
            at = block * HEIGHT
            re, im = (
                re * step_cos + im * step_sin + z[at : at + HEIGHT],
                im * step_cos - re * step_sin + z[SG + at : SG + at + HEIGHT],
            )
        re, im = re * cos + im * sin, im * cos - re * sin
        re = jnp.sum(re, 0, keepdims=True) * (1.0 / SG)
        im = jnp.sum(im, 0, keepdims=True) * (1.0 / SG)
        for tile in range(VB // M):
            at = chunk * (VB // M) + tile
            rows_out[at : at + 1, :] = re[:, tile * M : (tile + 1) * M]
            rows_out[NV // M + at : NV // M + at + 1, :] = im[:, tile * M : (tile + 1) * M]
    rows_out[OBS:, :] = tail[...]
    packed = rows_out[...].astype(BF)
    for peer in range(NT):
        out[peer] = packed


def grid_kernel(
    parts, col_t, row_fac, aterm, lift, k_right, phase, out, spread, res, slots
):
    part = parts[0].astype(F32)
    total = part[:OBS]
    slots[0] = part[OBS:]
    for peer in range(1, NT):
        part = parts[peer].astype(F32)
        total = total + part[:OBS]
        slots[peer] = part[OBS:]
    res[...] = total
    for tile in range(NV // M):
        t = tile // 2
        h = tile % 2
        weight = slots[t, 4 + h : 5 + h, :]
        r_re = weight * (slots[t, h : 1 + h, :] - res[tile : tile + 1, :])
        r_im = weight * (slots[t, 2 + h : 3 + h, :] - res[NV // M + tile : NV // M + tile + 1, :])
        span = slice(tile * M, (tile + 1) * M)
        cos, sin, step_cos, step_sin = row_factors(row_fac, span)
        re, im = r_re * cos - r_im * sin, r_re * sin + r_im * cos
        for block in range(STEPS):
            at = block * HEIGHT
            spread[at : at + HEIGHT, span] = re.astype(BF)
            spread[SG + at : SG + at + HEIGHT, span] = im.astype(BF)
            if block + 1 < STEPS:
                re, im = re * step_cos - im * step_sin, re * step_sin + im * step_cos
    both = dot_nt(spread[...], col_t[...])
    weight = aterm[...].astype(F32) * (1.0 / SG)
    g_re = (both[:SG, :SG] - both[SG:, SG:]) * weight
    g_im = (both[:SG, SG:] + both[SG:, :SG]) * weight
    grid = jnp.concatenate([g_re, g_im], 0).astype(BF)
    low = dot_tn(lift[...], grid).astype(BF)
    back = dot_nt(low, k_right[:, :SG])
    for f in range(NF):
        top = back[f * 16 : f * 16 + 8]
        bot = back[f * 16 + 8 : f * 16 + 16]
        re = top[:, :M] - bot[:, M:]
        im = bot[:, :M] + top[:, M:]
        cos = phase[0, f : f + 1, :]
        sin = phase[1, f : f + 1, :]
        both_parts = jnp.concatenate([re * cos + im * sin, im * cos - re * sin], 0).astype(BF)
        for b in range(NB):
            out[f * NB + b] = both_parts


def update_kernel(folded, w_rows, picks, turn, w_high, out, fs, os):
    count = NF * NB
    for s in range(count):
        fs[s * 2 * RD : (s + 1) * 2 * RD, :] = folded[s].astype(F32)
    mask = picks[...]
    columns = []
    for r in range(RD):
        pieces = []
        for part in range(2):
            value = fs[pl.ds(part * RD + r, count, stride=2 * RD), :]
            early = value * mask
            pieces.append(early)
            pieces.append(value - early)
        columns.append(jnp.concatenate(pieces, 0).astype(BF))
    stacked = jnp.concatenate(columns, 1)
    mixed = dot(w_rows[...], stacked)
    t_re = turn[0]
    t_im = turn[1]
    high = w_high[...]
    n_out = NH // NB
    for r in range(RD):
        y_re = mixed[:M, r * M : (r + 1) * M]
        y_im = mixed[M:, r * M : (r + 1) * M]
        z_re = (y_re * t_re - y_im * t_im).astype(BF)
        z_im = (y_re * t_im + y_im * t_re).astype(BF)
        os[pl.ds(r, 2 * n_out, stride=RD), :] = dot_nt(high, jnp.concatenate([z_re, z_im], 1))
    for part in range(2):
        for h in range(n_out):
            at = (part * n_out + h) * RD
            out[part, :, h * M : (h + 1) * M] = os[at : at + RD, :]


def shape(*dims, dtype=BF):
    return jax.ShapeDtypeStruct(dims, dtype)


SMEM = pl.BlockSpec(memory_space=pltpu.SMEM)
VMEM = pl.BlockSpec(memory_space=pltpu.VMEM)
HBM = pl.BlockSpec(memory_space=pltpu.HBM)
ANY = pl.BlockSpec(memory_space=pl.ANY)
PARAMS = pltpu.CompilerParams(vmem_limit_bytes=24 * 2**20)


def buf(*dims, dtype=BF):
    return pltpu.VMEM(dims, dtype)


def smem(*dims):
    return pltpu.SMEM(dims, jnp.int32)


def sems(count):
    return pltpu.SemaphoreType.DMA((count,))


def call(kernel, specs, outs, scratch, name, places=None, cost=None):
    single = not isinstance(outs, (list, tuple))
    return pl.pallas_call(
        kernel,
        out_shape=outs,
        in_specs=specs,
        out_specs=places or (VMEM if single else [VMEM] * len(outs)),
        scratch_shapes=scratch,
        compiler_params=PARAMS,
        cost_estimate=cost,
        name=name,
    )


def partner(value, mask):
    pairs = [(source, source ^ mask) for source in range(NT)]
    return lax.ppermute(value, "team", pairs)


def local(facet_rows, sub_offsets, facet_offsets, aterm, cells, observed, weights, counts):
    t = tables()
    offs = sub_offsets.T
    foffs = facet_offsets.T
    live = counts.transpose(1, 2, 0)
    keep = lambda array: pltpu.with_memory_space_constraint(array, pltpu.HBM)
    offs = keep(offs)
    foffs = keep(foffs)
    ids = [smem(2, NF * NB), smem(2, NF)]
    others = [partner(cells, mask) for mask in (1, 2, 3)]
    windows, offs_v, foffs_v, cells_v = call(
        forward_kernel,
        [HBM] * 6,
        [
            shape(NF, 2 * RD, M),
            shape(2, NF * NB, dtype=jnp.int32),
            shape(2, NF, dtype=jnp.int32),
            shape(NB, 2, VB, dtype=jnp.int32),
        ],
        [
            smem(2, NF * NB),
            buf(2, RD, L),
            buf(2 * M, 2 * NH),
            buf(2, M, M, dtype=F32),
            buf(2 * NH * RD, M, dtype=F32),
            buf(NF * 2 * RD, M, dtype=F32),
            sems(7),
        ],
        "windows",
    )(
        offs, foffs, keep(cells), keep(facet_rows),
        keep(t["fwd_rows"]), keep(t["fwd_turn"]),
    )
    *others, windows = lax.optimization_barrier((*others, windows))
    near = jnp.stack([part.reshape(NB, 2, VB) for part in [cells_v] + others])
    far = partner(near, NT // 2)
    arrived = lax.all_to_all(windows, "facet", 0, 0, tiled=True)
    col_t, row_fac, lift, k_right, own_map, tail, phase, w_rows, picks, turn, w_high = call(
        setup_kernel,
        [VMEM] * 2 + [ANY] * 2 + [HBM] * 7,
        [
            shape(2 * SG, NV),
            shape(24, NV, dtype=F32),
            shape(2 * SG, 2 * M),
            shape(2 * M, 2 * SG),
            shape(SG, SG),
            shape(SENT - OBS, M, dtype=F32),
            shape(2, NF, M, dtype=F32),
            shape(2 * M, 4 * NF * NB),
            shape(NF * NB, M, dtype=F32),
            shape(2, M, M, dtype=F32),
            shape(NH, 2 * M),
        ],
        ids
        + [smem(NB, NT, NF)]
        + [buf(NT // 2, 2, VB, dtype=jnp.int32)] * 2
        + [
            buf(2 * SG, 2 * M),
            buf(NT, 2, VB, dtype=jnp.int32),
            buf(2, VB),
            buf(2, VB),
            sems(11),
        ],
        "setup",
        cost=pl.CostEstimate(flops=20 * 10**9, transcendentals=0, bytes_accessed=2**22),
    )(
        offs_v, foffs_v, near, far, keep(t["k_left"]),
        keep(aterm), keep(observed), keep(weights.transpose(0, 2, 1, 3)),
        keep(live), keep(t["bwd_turn"]), keep(t["bwd_high"]),
    )
    parts = call(
        predict_kernel,
        [VMEM] * 8,
        shape(NT, SENT, M),
        [buf(SENT, M, dtype=F32)],
        "predict",
    )(arrived, lift, k_right, own_map, col_t, row_fac, tail, phase)
    gathered = lax.all_to_all(parts, "team", 0, 0, tiled=True)
    folded = call(
        grid_kernel,
        [VMEM] * 7,
        shape(NF * NB, 2 * RD, M),
        [
            buf(2 * SG, NV),
            buf(OBS, M, dtype=F32),
            buf(NT, SENT - OBS, M, dtype=F32),
        ],
        "grid",
    )(gathered, col_t, row_fac, own_map, lift, k_right, phase)
    returned = lax.all_to_all(folded, ("facet", "sub"), 0, 0, tiled=True)
    update = call(
        update_kernel,
        [VMEM] * 5,
        shape(2, RD, L // NB, dtype=F32),
        [buf(NF * NB * 2 * RD, M, dtype=F32), buf(NH * RD, M, dtype=F32)],
        "update",
    )(returned, w_rows, picks, turn, w_high)
    return update[None]


def solution(mesh):
    placed = (
        P("facet", None, "team", None),
        P(),
        P(),
        P("facet", None, None, None),
        P("facet", None, "team", None, None),
        P("facet", None, "team", None, None),
        P("facet", None, "team", None),
        P(),
    )
    return jax.shard_map(
        local,
        mesh=mesh,
        in_specs=placed,
        out_specs=P("facet", None, "team", "sub"),
        check_vma=False,
    )
```

```python
import math

import jax
import jax.numpy as jnp
import numpy as np
from jax import lax
from jax.experimental import pallas as pl
from jax.experimental.pallas import tpu as pltpu
from jax.sharding import PartitionSpec as P

L = 4096
M = 128
SG = 256
VB = 256
R = 64
NF = 16
NT = 8
NB = 2
RD = R // NT
NH = L // M
NV = NT * VB
TWO_PI = 2.0 * math.pi
BF = jnp.bfloat16
F32 = jnp.float32

ROOT = np.exp(2j * np.pi * np.arange(L) / L)


def wave(left, right, period, sign):
    steps = (np.outer(left, right) % period) * (L // period)
    table = ROOT[steps]
    return table if sign > 0 else table.conj()


def as_real(matrix):
    return np.block([[matrix.real, -matrix.imag], [matrix.imag, matrix.real]])


def half(matrix):
    return jnp.asarray(np.asarray(matrix, np.float32), BF)


def tables():
    lanes = np.arange(M)
    highs = np.arange(NH)
    fwd_rows = as_real(wave(lanes, highs, NH, -1))
    fwd_turn = wave(lanes, lanes, L, -1)
    bwd_turn = wave(lanes, lanes, L, 1) / math.sqrt(M)
    bwd_full = wave(highs, lanes, NH, 1)
    bwd_high = np.stack([as_real(part) for part in np.split(bwd_full, NB)])
    k_table = wave(lanes, np.arange(SG), SG, 1) / math.sqrt(M)
    k_left = as_real(k_table.T)
    return {
        "fwd_rows": half(fwd_rows),
        "fwd_turn": jnp.asarray(np.stack([fwd_turn.real, fwd_turn.imag]), F32),
        "bwd_turn": jnp.asarray(np.stack([bwd_turn.real, bwd_turn.imag]), F32),
        "bwd_high": half(bwd_high),
        "k_left": half(k_left),
    }


COS_TERMS = [(-1.0) ** n / math.factorial(2 * n) for n in range(9)]
SIN_TERMS = [(-1.0) ** n / math.factorial(2 * n + 1) for n in range(8)]


def turn_angle(steps, period):
    steps = steps & (period - 1)
    steps = jnp.where(steps >= period // 2, steps - period, steps)
    return steps.astype(F32) * (TWO_PI / period)


def series(square, terms):
    total = jnp.full_like(square, terms[-1])
    for term in terms[-2::-1]:
        total = total * square + term
    return total


def cos_of(angle):
    return series(angle * angle, COS_TERMS)


def sin_of(angle):
    return angle * series(angle * angle, SIN_TERMS)


def dot(left, right):
    return jnp.dot(left, right, preferred_element_type=F32)


def dot_tn(left, right):
    return lax.dot_general(left, right, (((0,), (0,)), ((), ())), preferred_element_type=F32)


def dot_nt(left, right):
    return lax.dot_general(left, right, (((1,), (1,)), ((), ())), preferred_element_type=F32)


def fetch(pairs, sems):
    copies = []
    for at, (source, target) in enumerate(pairs):
        copy = pltpu.make_async_copy(source, target, sems.at[at])
        copy.start()
        copies.append(copy)
    return copies


def forward_kernel(
    offs_h, foffs_h, cells_h, rows_h, w_rows_h, turn_h,
    out, offs_v, foffs_v, cells_v, offs, rows, w_rows, turn, xs, xo, sems,
):
    side = lax.axis_index("sub")
    copies = fetch(
        [
            (offs_h, offs),
            (rows_h.at[0], rows),
            (w_rows_h, w_rows),
            (turn_h, turn),
            (offs_h, offs_v),
            (foffs_h, foffs_v),
            (cells_h.at[0, :, 0], cells_v),
        ],
        sems,
    )
    copies[0].wait()
    row = lax.broadcasted_iota(jnp.int32, (NF, 2 * M), 0)
    lane = lax.broadcasted_iota(jnp.int32, (NF, 2 * M), 1)
    tuning = jnp.zeros((NF, 2 * M), jnp.int32)
    for a in range(NF):
        tuning = jnp.where(row == a, offs[1, a * NB + side], tuning)
    pick = lane[:, :M] >= (tuning[:, :M] & (M - 1))
    first = (tuning >> 7) * (lane & (M - 1))
    later = lane & (M - 1)
    blocks = []
    for part in range(2):
        for late in range(2):
            steps = (L // NH) * (first + late * later) + (L // 4) * (part - (lane >> 7))
            blocks.append((cos_of(turn_angle(steps, L)) * (1.0 / 64.0)).astype(BF))
    w_high = jnp.concatenate(blocks, 0)
    for copy in copies[1:]:
        copy.wait()
    for part in range(2):
        whole = rows[part].astype(F32)
        for high in range(NH):
            xs[pl.ds((part * NH + high) * RD, RD), :] = whole[:, high * M : (high + 1) * M]
    stacked = jnp.concatenate(
        [xs[pl.ds(r, 2 * NH, stride=RD), :].astype(BF) for r in range(RD)], 1
    )
    mixed = dot(w_rows[...], stacked)
    t_re = turn[0]
    t_im = turn[1]
    for r in range(RD):
        y_re = mixed[:M, r * M : (r + 1) * M]
        y_im = mixed[M:, r * M : (r + 1) * M]
        z_re = (y_re * t_re - y_im * t_im).astype(BF)
        z_im = (y_re * t_im + y_im * t_re).astype(BF)
        found = dot_nt(w_high, jnp.concatenate([z_re, z_im], 1))
        for part in range(2):
            at = part * 2 * NF
            value = jnp.where(pick, found[at : at + NF], found[at + NF : at + 2 * NF])
            xo[pl.ds(part * RD + r, NF, stride=2 * RD), :] = value
    for a in range(NF):
        out[a] = xo[a * 2 * RD : (a + 1) * 2 * RD, :].astype(BF)


SENT = 40
OBS = 2 * NV // M
HEIGHT = 16
STEPS = SG // HEIGHT


def setup_kernel(
    offs_v, foffs_v, near_h, far_h, k_left_h, aterm_h, seen_h, weights_h, counts_h, turn_h, w_high_h,
    col_t, row_fac, lift, k_right, aterm, tail, phase, w_rows, picks, turn, w_high,
    offs, foffs, counts, near, far, k_left, spots, seen, weights, sems,
):
    facet = lax.axis_index("facet")
    team = lax.axis_index("team")
    side = lax.axis_index("sub")
    copies = fetch(
        [
            (offs_v, offs),
            (foffs_v, foffs),
            (k_left_h, k_left),
            (near_h.at[:, side], near),
            (far_h.at[:, side], far),
            (aterm_h.at[0, side], aterm),
            (seen_h.at[0, side, 0], seen),
            (weights_h.at[0, 0], weights),
            (counts_h, counts),
            (turn_h, turn),
            (w_high_h.at[side], w_high),
        ],
        sems,
    )
    for copy in copies[:2]:
        copy.wait()
    shift_u = offs[0, facet * NB + side]
    row = lax.broadcasted_iota(jnp.int32, (2 * RD, 2 * M), 0)
    lane = lax.broadcasted_iota(jnp.int32, (2 * RD, 2 * M), 1)
    p = lane & (M - 1)
    quarter = ((row >> 3) - (lane >> 7)) * (L // 4)
    row_turn = (L // R) * (p + shift_u) * (team * RD + (row & (RD - 1)))
    base = quarter - row_turn
    blocks = []
    for f in range(NF):
        steps = base + p * foffs[0, f]
        blocks.append((cos_of(turn_angle(steps, L)) * (1.0 / 32.0)).astype(BF))
    joined = jnp.concatenate(blocks, 0)
    own = offs[1, facet * NB + side]
    row = lax.broadcasted_iota(jnp.int32, (NF, M), 0)
    lane = lax.broadcasted_iota(jnp.int32, (NF, M), 1)
    column = jnp.zeros((NF, M), jnp.int32)
    for f in range(NF):
        column = jnp.where(row == f, foffs[1, f], column)
    angle = turn_angle(column * ((lane - own) & (M - 1)), L)
    phase[0] = cos_of(angle)
    phase[1] = sin_of(angle)
    row = lax.broadcasted_iota(jnp.int32, (M, SG), 0)
    lane = lax.broadcasted_iota(jnp.int32, (M, SG), 1)
    angle = turn_angle(((row - own) & (M - 1)) * lane, SG)
    k_re = (cos_of(angle) * (1.0 / math.sqrt(M))).astype(BF)
    k_im = (sin_of(angle) * (1.0 / math.sqrt(M))).astype(BF)
    k_right[:M, :SG] = k_re
    k_right[:M, SG:] = k_im
    k_right[M:, :SG] = -k_im
    k_right[M:, SG:] = k_re
    lane = lax.broadcasted_iota(jnp.int32, (8, M), 1)
    row = lax.broadcasted_iota(jnp.int32, (NF * NB, M), 0)
    high = jnp.zeros((8, M), jnp.int32)
    low = jnp.zeros((NF * NB, M), jnp.int32)
    for s in range(NF * NB):
        high = jnp.where((lane & (NF * NB - 1)) == s, offs[1, s] >> 7, high)
        low = jnp.where(row == s, offs[1, s] & (M - 1), low)
    lane_rows = lax.broadcasted_iota(jnp.int32, (NF * NB, M), 1)
    picks[...] = jnp.where(lane_rows >= low, 1.0, 0.0)
    high = high + ((lane >> 5) & 1)
    quarter = (lane >> 6) * (L // 4)
    high = jnp.concatenate([high] * 4, 0)
    quarter = jnp.concatenate([quarter] * 4, 0)
    for block in range(2 * M // 32):
        spot = lax.broadcasted_iota(jnp.int32, (32, M), 0) + block * 32
        steps = (L // NH) * (spot & (M - 1)) * high + quarter - (spot >> 7) * (L // 4)
        w_rows[block * 32 : (block + 1) * 32, :] = cos_of(turn_angle(steps, L)).astype(BF)
    for copy in copies[2:]:
        copy.wait()
    lift[...] = dot_nt(k_left[...], joined).astype(BF)
    pair = weights[...].astype(F32)
    weight = jnp.where(side == 0, pair[0:1], pair[1:2])
    slot = lax.broadcasted_iota(jnp.int32, (1, VB), 1)
    weight = jnp.where(slot < counts[side, team, facet], weight, 0.0)
    both = seen[...].astype(F32)
    tail[...] = jnp.zeros_like(tail)
    for at in range(2):
        half = slice(at * M, (at + 1) * M)
        tail[at : at + 1, :] = both[0:1, half]
        tail[2 + at : 3 + at, :] = both[1:2, half]
        tail[4 + at : 5 + at, :] = weight[:, half]
    for step in range(NT // 2):
        spots[team ^ step] = near[step]
        spots[team ^ (NT - 1) ^ step] = far[step]
    count = lax.broadcasted_iota(jnp.int32, (8, M), 0)

    def turns(place, tile):
        half = slice(tile % 2 * M, (tile % 2 + 1) * M)
        spot = jnp.broadcast_to(spots[tile // 2, place : place + 1, half], (8, M))
        angle = turn_angle(spot * count, 4 * SG)
        step = turn_angle(spot * 8, 4 * SG)
        return cos_of(angle), sin_of(angle), cos_of(step), sin_of(step)

    for tile in range(NV // M):
        lanes = slice(tile * M, (tile + 1) * M)
        cos, sin, step_cos, step_sin = turns(0, tile)
        row_fac[0:8, lanes] = cos
        row_fac[8:16, lanes] = sin
        row_fac[16:17, lanes] = step_cos[0:1]
        row_fac[17:18, lanes] = step_sin[0:1]
        cos, sin, step_cos, step_sin = widen(*turns(1, tile))
        for block in range(STEPS):
            at = block * HEIGHT
            col_t[at : at + HEIGHT, lanes] = cos.astype(BF)
            col_t[SG + at : SG + at + HEIGHT, lanes] = sin.astype(BF)
            if block + 1 < STEPS:
                cos, sin = cos * step_cos - sin * step_sin, cos * step_sin + sin * step_cos


def widen(cos, sin, step_cos, step_sin):
    far_cos = cos * step_cos - sin * step_sin
    far_sin = cos * step_sin + sin * step_cos
    twice_cos = step_cos * step_cos - step_sin * step_sin
    twice_sin = 2.0 * step_cos * step_sin
    return (
        jnp.concatenate([cos, far_cos], 0),
        jnp.concatenate([sin, far_sin], 0),
        twice(twice_cos),
        twice(twice_sin),
    )


def row_factors(row_fac, span):
    width = span.stop - span.start
    return widen(
        row_fac[0:8, span],
        row_fac[8:16, span],
        jnp.broadcast_to(row_fac[16:17, span], (8, width)),
        jnp.broadcast_to(row_fac[17:18, span], (8, width)),
    )


def twice(value):
    return jnp.concatenate([value, value], 0)


def predict_kernel(
    spec, lift, k_right, aterm, col_t, row_fac, tail, phase, out, rows_out
):
    parts = []
    for f in range(NF):
        both = spec[f].astype(F32)
        cos = phase[0, f : f + 1, :]
        sin = phase[1, f : f + 1, :]
        parts.append(both[:RD] * cos - both[RD:] * sin)
        parts.append(both[:RD] * sin + both[RD:] * cos)
    turned = dot(lift[...], jnp.concatenate(parts, 0).astype(BF)).astype(BF)
    image = dot(jnp.concatenate([turned[:SG], turned[SG:]], 1), k_right[...])
    weight = aterm[...].astype(F32)
    w_re = image[:, :SG] * weight
    w_im = image[:, SG:] * weight
    left = jnp.concatenate(
        [
            jnp.concatenate([w_re, w_im], 1).astype(BF),
            jnp.concatenate([w_im, -w_re], 1).astype(BF),
        ],
        0,
    )
    for chunk in range(NT):
        span = slice(chunk * VB, (chunk + 1) * VB)
        z = dot(left, col_t[:, span])
        cos, sin, step_cos, step_sin = row_factors(row_fac, span)
        re = z[SG - HEIGHT : SG]
        im = z[2 * SG - HEIGHT :]
        for block in range(STEPS - 2, -1, -1):
            at = block * HEIGHT
            re, im = (
                re * step_cos + im * step_sin + z[at : at + HEIGHT],
                im * step_cos - re * step_sin + z[SG + at : SG + at + HEIGHT],
            )
        re, im = re * cos + im * sin, im * cos - re * sin
        re = jnp.sum(re, 0, keepdims=True) * (1.0 / SG)
        im = jnp.sum(im, 0, keepdims=True) * (1.0 / SG)
        for tile in range(VB // M):
            at = chunk * (VB // M) + tile
            rows_out[at : at + 1, :] = re[:, tile * M : (tile + 1) * M]
            rows_out[NV // M + at : NV // M + at + 1, :] = im[:, tile * M : (tile + 1) * M]
    rows_out[OBS:, :] = tail[...]
    packed = rows_out[...].astype(BF)
    for peer in range(NT):
        out[peer] = packed


def grid_kernel(
    parts, col_t, row_fac, aterm, lift, k_right, phase, out, spread, res, slots
):
    part = parts[0].astype(F32)
    total = part[:OBS]
    slots[0] = part[OBS:]
    for peer in range(1, NT):
        part = parts[peer].astype(F32)
        total = total + part[:OBS]
        slots[peer] = part[OBS:]
    res[...] = total
    for tile in range(NV // M):
        t = tile // 2
        h = tile % 2
        weight = slots[t, 4 + h : 5 + h, :]
        r_re = weight * (slots[t, h : 1 + h, :] - res[tile : tile + 1, :])
        r_im = weight * (slots[t, 2 + h : 3 + h, :] - res[NV // M + tile : NV // M + tile + 1, :])
        span = slice(tile * M, (tile + 1) * M)
        cos, sin, step_cos, step_sin = row_factors(row_fac, span)
        re, im = r_re * cos - r_im * sin, r_re * sin + r_im * cos
        for block in range(STEPS):
            at = block * HEIGHT
            spread[at : at + HEIGHT, span] = re.astype(BF)
            spread[SG + at : SG + at + HEIGHT, span] = im.astype(BF)
            if block + 1 < STEPS:
                re, im = re * step_cos - im * step_sin, re * step_sin + im * step_cos
    both = dot_nt(spread[...], col_t[...])
    weight = aterm[...].astype(F32) * (1.0 / SG)
    g_re = (both[:SG, :SG] - both[SG:, SG:]) * weight
    g_im = (both[:SG, SG:] + both[SG:, :SG]) * weight
    grid = jnp.concatenate([g_re, g_im], 0).astype(BF)
    low = dot_tn(lift[...], grid).astype(BF)
    back = dot_nt(low, k_right[:, :SG])
    for f in range(NF):
        top = back[f * 16 : f * 16 + 8]
        bot = back[f * 16 + 8 : f * 16 + 16]
        re = top[:, :M] - bot[:, M:]
        im = bot[:, :M] + top[:, M:]
        cos = phase[0, f : f + 1, :]
        sin = phase[1, f : f + 1, :]
        both_parts = jnp.concatenate([re * cos + im * sin, im * cos - re * sin], 0).astype(BF)
        for b in range(NB):
            out[f * NB + b] = both_parts


def update_kernel(folded, w_rows, picks, turn, w_high, out, fs, os):
    count = NF * NB
    for s in range(count):
        fs[s * 2 * RD : (s + 1) * 2 * RD, :] = folded[s].astype(F32)
    mask = picks[...]
    columns = []
    for r in range(RD):
        pieces = []
        for part in range(2):
            value = fs[pl.ds(part * RD + r, count, stride=2 * RD), :]
            early = value * mask
            pieces.append(early)
            pieces.append(value - early)
        columns.append(jnp.concatenate(pieces, 0).astype(BF))
    stacked = jnp.concatenate(columns, 1)
    mixed = dot(w_rows[...], stacked)
    t_re = turn[0]
    t_im = turn[1]
    high = w_high[...]
    n_out = NH // NB
    for r in range(RD):
        y_re = mixed[:M, r * M : (r + 1) * M]
        y_im = mixed[M:, r * M : (r + 1) * M]
        z_re = (y_re * t_re - y_im * t_im).astype(BF)
        z_im = (y_re * t_im + y_im * t_re).astype(BF)
        os[pl.ds(r, 2 * n_out, stride=RD), :] = dot_nt(high, jnp.concatenate([z_re, z_im], 1))
    for part in range(2):
        for h in range(n_out):
            at = (part * n_out + h) * RD
            out[part, :, h * M : (h + 1) * M] = os[at : at + RD, :]


def shape(*dims, dtype=BF):
    return jax.ShapeDtypeStruct(dims, dtype)


SMEM = pl.BlockSpec(memory_space=pltpu.SMEM)
VMEM = pl.BlockSpec(memory_space=pltpu.VMEM)
HBM = pl.BlockSpec(memory_space=pltpu.HBM)
ANY = pl.BlockSpec(memory_space=pl.ANY)
PARAMS = pltpu.CompilerParams(vmem_limit_bytes=24 * 2**20)


def buf(*dims, dtype=BF):
    return pltpu.VMEM(dims, dtype)


def smem(*dims):
    return pltpu.SMEM(dims, jnp.int32)


def sems(count):
    return pltpu.SemaphoreType.DMA((count,))


def call(kernel, specs, outs, scratch, name, places=None, cost=None):
    single = not isinstance(outs, (list, tuple))
    return pl.pallas_call(
        kernel,
        out_shape=outs,
        in_specs=specs,
        out_specs=places or (VMEM if single else [VMEM] * len(outs)),
        scratch_shapes=scratch,
        compiler_params=PARAMS,
        cost_estimate=cost,
        name=name,
    )


def partner(value, mask):
    pairs = [(source, source ^ mask) for source in range(NT)]
    return lax.ppermute(value, "team", pairs)


def local(facet_rows, sub_offsets, facet_offsets, aterm, cells, observed, weights, counts):
    t = tables()
    offs = sub_offsets.T
    foffs = facet_offsets.T
    live = counts.transpose(1, 2, 0)
    keep = lambda array: pltpu.with_memory_space_constraint(array, pltpu.HBM)
    offs = keep(offs)
    foffs = keep(foffs)
    ids = [smem(2, NF * NB), smem(2, NF)]
    others = [partner(cells, mask) for mask in (1, 2, 3)]
    windows, offs_v, foffs_v, cells_v = call(
        forward_kernel,
        [HBM] * 6,
        [
            shape(NF, 2 * RD, M),
            shape(2, NF * NB, dtype=jnp.int32),
            shape(2, NF, dtype=jnp.int32),
            shape(NB, 2, VB, dtype=jnp.int32),
        ],
        [
            smem(2, NF * NB),
            buf(2, RD, L),
            buf(2 * M, 2 * NH),
            buf(2, M, M, dtype=F32),
            buf(2 * NH * RD, M, dtype=F32),
            buf(NF * 2 * RD, M, dtype=F32),
            sems(7),
        ],
        "windows",
    )(
        offs, foffs, keep(cells), keep(facet_rows),
        keep(t["fwd_rows"]), keep(t["fwd_turn"]),
    )
    *others, windows = lax.optimization_barrier((*others, windows))
    near = jnp.stack([part.reshape(NB, 2, VB) for part in [cells_v] + others])
    far = partner(near, NT - 1)
    arrived = lax.all_to_all(windows, "facet", 0, 0, tiled=True)
    col_t, row_fac, lift, k_right, own_map, tail, phase, w_rows, picks, turn, w_high = call(
        setup_kernel,
        [VMEM] * 2 + [ANY] * 2 + [HBM] * 7,
        [
            shape(2 * SG, NV),
            shape(24, NV, dtype=F32),
            shape(2 * SG, 2 * M),
            shape(2 * M, 2 * SG),
            shape(SG, SG),
            shape(SENT - OBS, M, dtype=F32),
            shape(2, NF, M, dtype=F32),
            shape(2 * M, 4 * NF * NB),
            shape(NF * NB, M, dtype=F32),
            shape(2, M, M, dtype=F32),
            shape(NH, 2 * M),
        ],
        ids
        + [smem(NB, NT, NF)]
        + [buf(NT // 2, 2, VB, dtype=jnp.int32)] * 2
        + [
            buf(2 * SG, 2 * M),
            buf(NT, 2, VB, dtype=jnp.int32),
            buf(2, VB),
            buf(2, VB),
            sems(11),
        ],
        "setup",
        cost=pl.CostEstimate(flops=20 * 10**9, transcendentals=0, bytes_accessed=2**22),
    )(
        offs_v, foffs_v, near, far, keep(t["k_left"]),
        keep(aterm), keep(observed), keep(weights.transpose(0, 2, 1, 3)),
        keep(live), keep(t["bwd_turn"]), keep(t["bwd_high"]),
    )
    parts = call(
        predict_kernel,
        [VMEM] * 8,
        shape(NT, SENT, M),
        [buf(SENT, M, dtype=F32)],
        "predict",
    )(arrived, lift, k_right, own_map, col_t, row_fac, tail, phase)
    gathered = lax.all_to_all(parts, "team", 0, 0, tiled=True)
    folded = call(
        grid_kernel,
        [VMEM] * 7,
        shape(NF * NB, 2 * RD, M),
        [
            buf(2 * SG, NV),
            buf(OBS, M, dtype=F32),
            buf(NT, SENT - OBS, M, dtype=F32),
        ],
        "grid",
    )(gathered, col_t, row_fac, own_map, lift, k_right, phase)
    returned = lax.all_to_all(folded, ("facet", "sub"), 0, 0, tiled=True)
    update = call(
        update_kernel,
        [VMEM] * 5,
        shape(2, RD, L // NB, dtype=F32),
        [buf(NF * NB * 2 * RD, M, dtype=F32), buf(NH * RD, M, dtype=F32)],
        "update",
    )(returned, w_rows, picks, turn, w_high)
    return update[None]


def solution(mesh):
    placed = (
        P("facet", None, "team", None),
        P(),
        P(),
        P("facet", None, None, None),
        P("facet", None, "team", None, None),
        P("facet", None, "team", None, None),
        P("facet", None, "team", None),
        P(),
    )
    return jax.shard_map(
        local,
        mesh=mesh,
        in_specs=placed,
        out_specs=P("facet", None, "team", "sub"),
        check_vma=False,
    )
```

```python
import math

import jax
import jax.numpy as jnp
import numpy as np
from jax import lax
from jax.experimental import pallas as pl
from jax.experimental.pallas import tpu as pltpu
from jax.sharding import PartitionSpec as P

L = 4096
M = 128
SG = 256
VB = 256
R = 64
NF = 16
NT = 8
NB = 2
RD = R // NT
NH = L // M
NV = NT * VB
TWO_PI = 2.0 * math.pi
NEAR = (0, 1, 2, 3)
FAR = 6
BF = jnp.bfloat16
F32 = jnp.float32

ROOT = np.exp(2j * np.pi * np.arange(L) / L)


def wave(left, right, period, sign):
    steps = (np.outer(left, right) % period) * (L // period)
    table = ROOT[steps]
    return table if sign > 0 else table.conj()


def as_real(matrix):
    return np.block([[matrix.real, -matrix.imag], [matrix.imag, matrix.real]])


def half(matrix):
    return jnp.asarray(np.asarray(matrix, np.float32), BF)


def tables():
    lanes = np.arange(M)
    highs = np.arange(NH)
    fwd_rows = as_real(wave(lanes, highs, NH, -1))
    fwd_turn = wave(lanes, lanes, L, -1)
    bwd_turn = wave(lanes, lanes, L, 1) / math.sqrt(M)
    bwd_full = wave(highs, lanes, NH, 1)
    bwd_high = np.stack([as_real(part) for part in np.split(bwd_full, NB)])
    k_table = wave(lanes, np.arange(SG), SG, 1) / math.sqrt(M)
    k_left = as_real(k_table.T)
    return {
        "fwd_rows": half(fwd_rows),
        "fwd_turn": jnp.asarray(np.stack([fwd_turn.real, fwd_turn.imag]), F32),
        "bwd_turn": jnp.asarray(np.stack([bwd_turn.real, bwd_turn.imag]), F32),
        "bwd_high": half(bwd_high),
        "k_left": half(k_left),
    }


COS_TERMS = [(-1.0) ** n / math.factorial(2 * n) for n in range(9)]
SIN_TERMS = [(-1.0) ** n / math.factorial(2 * n + 1) for n in range(8)]


def turn_angle(steps, period):
    steps = steps & (period - 1)
    steps = jnp.where(steps >= period // 2, steps - period, steps)
    return steps.astype(F32) * (TWO_PI / period)


def series(square, terms):
    total = jnp.full_like(square, terms[-1])
    for term in terms[-2::-1]:
        total = total * square + term
    return total


def cos_of(angle):
    return series(angle * angle, COS_TERMS)


def sin_of(angle):
    return angle * series(angle * angle, SIN_TERMS)


def dot(left, right):
    return jnp.dot(left, right, preferred_element_type=F32)


def dot_tn(left, right):
    return lax.dot_general(left, right, (((0,), (0,)), ((), ())), preferred_element_type=F32)


def dot_nt(left, right):
    return lax.dot_general(left, right, (((1,), (1,)), ((), ())), preferred_element_type=F32)


def fetch(pairs, sems):
    copies = []
    for at, (source, target) in enumerate(pairs):
        copy = pltpu.make_async_copy(source, target, sems.at[at])
        copy.start()
        copies.append(copy)
    return copies


def forward_kernel(
    offs_h, foffs_h, cells_h, rows_h, w_rows_h, turn_h,
    out, offs_v, foffs_v, cells_v, offs, rows, w_rows, turn, xs, xo, sems,
):
    side = lax.axis_index("sub")
    copies = fetch(
        [
            (offs_h, offs),
            (rows_h.at[0], rows),
            (w_rows_h, w_rows),
            (turn_h, turn),
            (offs_h, offs_v),
            (foffs_h, foffs_v),
            (cells_h.at[0, :, 0], cells_v),
        ],
        sems,
    )
    copies[0].wait()
    row = lax.broadcasted_iota(jnp.int32, (NF, 2 * M), 0)
    lane = lax.broadcasted_iota(jnp.int32, (NF, 2 * M), 1)
    tuning = jnp.zeros((NF, 2 * M), jnp.int32)
    for a in range(NF):
        tuning = jnp.where(row == a, offs[1, a * NB + side], tuning)
    pick = lane[:, :M] >= (tuning[:, :M] & (M - 1))
    first = (tuning >> 7) * (lane & (M - 1))
    later = lane & (M - 1)
    blocks = []
    for part in range(2):
        for late in range(2):
            steps = (L // NH) * (first + late * later) + (L // 4) * (part - (lane >> 7))
            blocks.append((cos_of(turn_angle(steps, L)) * (1.0 / 64.0)).astype(BF))
    w_high = jnp.concatenate(blocks, 0)
    for copy in copies[1:]:
        copy.wait()
    for part in range(2):
        whole = rows[part].astype(F32)
        for high in range(NH):
            xs[pl.ds((part * NH + high) * RD, RD), :] = whole[:, high * M : (high + 1) * M]
    stacked = jnp.concatenate(
        [xs[pl.ds(r, 2 * NH, stride=RD), :].astype(BF) for r in range(RD)], 1
    )
    mixed = dot(w_rows[...], stacked)
    t_re = turn[0]
    t_im = turn[1]
    for r in range(RD):
        y_re = mixed[:M, r * M : (r + 1) * M]
        y_im = mixed[M:, r * M : (r + 1) * M]
        z_re = (y_re * t_re - y_im * t_im).astype(BF)
        z_im = (y_re * t_im + y_im * t_re).astype(BF)
        found = dot_nt(w_high, jnp.concatenate([z_re, z_im], 1))
        for part in range(2):
            at = part * 2 * NF
            value = jnp.where(pick, found[at : at + NF], found[at + NF : at + 2 * NF])
            xo[pl.ds(part * RD + r, NF, stride=2 * RD), :] = value
    for a in range(NF):
        out[a] = xo[a * 2 * RD : (a + 1) * 2 * RD, :].astype(BF)


SENT = 40
OBS = 2 * NV // M
HEIGHT = 16
STEPS = SG // HEIGHT


def setup_kernel(
    offs_v, foffs_v, near_h, far_h, k_left_h, aterm_h, seen_h, weights_h, counts_h, turn_h, w_high_h,
    col_t, row_fac, lift, k_right, aterm, tail, phase, w_rows, picks, turn, w_high,
    offs, foffs, counts, near, far, k_left, spots, seen, weights, sems,
):
    facet = lax.axis_index("facet")
    team = lax.axis_index("team")
    side = lax.axis_index("sub")
    copies = fetch(
        [
            (offs_v, offs),
            (foffs_v, foffs),
            (k_left_h, k_left),
            (near_h.at[:, side], near),
            (far_h.at[:, side], far),
            (aterm_h.at[0, side], aterm),
            (seen_h.at[0, side, 0], seen),
            (weights_h.at[0, 0], weights),
            (counts_h, counts),
            (turn_h, turn),
            (w_high_h.at[side], w_high),
        ],
        sems,
    )
    for copy in copies[:2]:
        copy.wait()
    shift_u = offs[0, facet * NB + side]
    row = lax.broadcasted_iota(jnp.int32, (2 * RD, 2 * M), 0)
    lane = lax.broadcasted_iota(jnp.int32, (2 * RD, 2 * M), 1)
    p = lane & (M - 1)
    quarter = ((row >> 3) - (lane >> 7)) * (L // 4)
    row_turn = (L // R) * (p + shift_u) * (team * RD + (row & (RD - 1)))
    base = quarter - row_turn
    blocks = []
    for f in range(NF):
        steps = base + p * foffs[0, f]
        blocks.append((cos_of(turn_angle(steps, L)) * (1.0 / 32.0)).astype(BF))
    joined = jnp.concatenate(blocks, 0)
    own = offs[1, facet * NB + side]
    row = lax.broadcasted_iota(jnp.int32, (NF, M), 0)
    lane = lax.broadcasted_iota(jnp.int32, (NF, M), 1)
    column = jnp.zeros((NF, M), jnp.int32)
    for f in range(NF):
        column = jnp.where(row == f, foffs[1, f], column)
    angle = turn_angle(column * ((lane - own) & (M - 1)), L)
    phase[0] = cos_of(angle)
    phase[1] = sin_of(angle)
    row = lax.broadcasted_iota(jnp.int32, (M, SG), 0)
    lane = lax.broadcasted_iota(jnp.int32, (M, SG), 1)
    angle = turn_angle(((row - own) & (M - 1)) * lane, SG)
    k_re = (cos_of(angle) * (1.0 / math.sqrt(M))).astype(BF)
    k_im = (sin_of(angle) * (1.0 / math.sqrt(M))).astype(BF)
    k_right[:M, :SG] = k_re
    k_right[:M, SG:] = k_im
    k_right[M:, :SG] = -k_im
    k_right[M:, SG:] = k_re
    lane = lax.broadcasted_iota(jnp.int32, (8, M), 1)
    row = lax.broadcasted_iota(jnp.int32, (NF * NB, M), 0)
    high = jnp.zeros((8, M), jnp.int32)
    low = jnp.zeros((NF * NB, M), jnp.int32)
    for s in range(NF * NB):
        high = jnp.where((lane & (NF * NB - 1)) == s, offs[1, s] >> 7, high)
        low = jnp.where(row == s, offs[1, s] & (M - 1), low)
    lane_rows = lax.broadcasted_iota(jnp.int32, (NF * NB, M), 1)
    picks[...] = jnp.where(lane_rows >= low, 1.0, 0.0)
    high = high + ((lane >> 5) & 1)
    quarter = (lane >> 6) * (L // 4)
    high = jnp.concatenate([high] * 4, 0)
    quarter = jnp.concatenate([quarter] * 4, 0)
    for block in range(2 * M // 32):
        spot = lax.broadcasted_iota(jnp.int32, (32, M), 0) + block * 32
        steps = (L // NH) * (spot & (M - 1)) * high + quarter - (spot >> 7) * (L // 4)
        w_rows[block * 32 : (block + 1) * 32, :] = cos_of(turn_angle(steps, L)).astype(BF)
    for copy in copies[2:]:
        copy.wait()
    lift[...] = dot_nt(k_left[...], joined).astype(BF)
    pair = weights[...].astype(F32)
    weight = jnp.where(side == 0, pair[0:1], pair[1:2])
    slot = lax.broadcasted_iota(jnp.int32, (1, VB), 1)
    weight = jnp.where(slot < counts[side, team, facet], weight, 0.0)
    both = seen[...].astype(F32)
    tail[...] = jnp.zeros_like(tail)
    for at in range(2):
        half = slice(at * M, (at + 1) * M)
        tail[at : at + 1, :] = both[0:1, half]
        tail[2 + at : 3 + at, :] = both[1:2, half]
        tail[4 + at : 5 + at, :] = weight[:, half]
    for at, mask in enumerate(NEAR):
        spots[team ^ mask] = near[at]
        spots[team ^ FAR ^ mask] = far[at]
    count = lax.broadcasted_iota(jnp.int32, (8, M), 0)

    def turns(place, tile):
        half = slice(tile % 2 * M, (tile % 2 + 1) * M)
        spot = jnp.broadcast_to(spots[tile // 2, place : place + 1, half], (8, M))
        angle = turn_angle(spot * count, 4 * SG)
        step = turn_angle(spot * 8, 4 * SG)
        return cos_of(angle), sin_of(angle), cos_of(step), sin_of(step)

    for tile in range(NV // M):
        lanes = slice(tile * M, (tile + 1) * M)
        cos, sin, step_cos, step_sin = turns(0, tile)
        row_fac[0:8, lanes] = cos
        row_fac[8:16, lanes] = sin
        row_fac[16:17, lanes] = step_cos[0:1]
        row_fac[17:18, lanes] = step_sin[0:1]
        cos, sin, step_cos, step_sin = widen(*turns(1, tile))
        for block in range(STEPS):
            at = block * HEIGHT
            col_t[at : at + HEIGHT, lanes] = cos.astype(BF)
            col_t[SG + at : SG + at + HEIGHT, lanes] = sin.astype(BF)
            if block + 1 < STEPS:
                cos, sin = cos * step_cos - sin * step_sin, cos * step_sin + sin * step_cos


def widen(cos, sin, step_cos, step_sin):
    far_cos = cos * step_cos - sin * step_sin
    far_sin = cos * step_sin + sin * step_cos
    twice_cos = step_cos * step_cos - step_sin * step_sin
    twice_sin = 2.0 * step_cos * step_sin
    return (
        jnp.concatenate([cos, far_cos], 0),
        jnp.concatenate([sin, far_sin], 0),
        twice(twice_cos),
        twice(twice_sin),
    )


def row_factors(row_fac, span):
    width = span.stop - span.start
    return widen(
        row_fac[0:8, span],
        row_fac[8:16, span],
        jnp.broadcast_to(row_fac[16:17, span], (8, width)),
        jnp.broadcast_to(row_fac[17:18, span], (8, width)),
    )


def twice(value):
    return jnp.concatenate([value, value], 0)


def predict_kernel(
    spec, lift, k_right, aterm, col_t, row_fac, tail, phase, out, rows_out
):
    parts = []
    for f in range(NF):
        both = spec[f].astype(F32)
        cos = phase[0, f : f + 1, :]
        sin = phase[1, f : f + 1, :]
        parts.append(both[:RD] * cos - both[RD:] * sin)
        parts.append(both[:RD] * sin + both[RD:] * cos)
    turned = dot(lift[...], jnp.concatenate(parts, 0).astype(BF)).astype(BF)
    image = dot(jnp.concatenate([turned[:SG], turned[SG:]], 1), k_right[...])
    weight = aterm[...].astype(F32)
    w_re = image[:, :SG] * weight
    w_im = image[:, SG:] * weight
    left = jnp.concatenate(
        [
            jnp.concatenate([w_re, w_im], 1).astype(BF),
            jnp.concatenate([w_im, -w_re], 1).astype(BF),
        ],
        0,
    )
    for chunk in range(NT):
        span = slice(chunk * VB, (chunk + 1) * VB)
        z = dot(left, col_t[:, span])
        cos, sin, step_cos, step_sin = row_factors(row_fac, span)
        re = z[SG - HEIGHT : SG]
        im = z[2 * SG - HEIGHT :]
        for block in range(STEPS - 2, -1, -1):
            at = block * HEIGHT
            re, im = (
                re * step_cos + im * step_sin + z[at : at + HEIGHT],
                im * step_cos - re * step_sin + z[SG + at : SG + at + HEIGHT],
            )
        re, im = re * cos + im * sin, im * cos - re * sin
        re = jnp.sum(re, 0, keepdims=True) * (1.0 / SG)
        im = jnp.sum(im, 0, keepdims=True) * (1.0 / SG)
        for tile in range(VB // M):
            at = chunk * (VB // M) + tile
            rows_out[at : at + 1, :] = re[:, tile * M : (tile + 1) * M]
            rows_out[NV // M + at : NV // M + at + 1, :] = im[:, tile * M : (tile + 1) * M]
    rows_out[OBS:, :] = tail[...]
    packed = rows_out[...].astype(BF)
    for peer in range(NT):
        out[peer] = packed


def grid_kernel(
    parts, col_t, row_fac, aterm, lift, k_right, phase, out, spread, res, slots
):
    part = parts[0].astype(F32)
    total = part[:OBS]
    slots[0] = part[OBS:]
    for peer in range(1, NT):
        part = parts[peer].astype(F32)
        total = total + part[:OBS]
        slots[peer] = part[OBS:]
    res[...] = total
    for tile in range(NV // M):
        t = tile // 2
        h = tile % 2
        weight = slots[t, 4 + h : 5 + h, :]
        r_re = weight * (slots[t, h : 1 + h, :] - res[tile : tile + 1, :])
        r_im = weight * (slots[t, 2 + h : 3 + h, :] - res[NV // M + tile : NV // M + tile + 1, :])
        span = slice(tile * M, (tile + 1) * M)
        cos, sin, step_cos, step_sin = row_factors(row_fac, span)
        re, im = r_re * cos - r_im * sin, r_re * sin + r_im * cos
        for block in range(STEPS):
            at = block * HEIGHT
            spread[at : at + HEIGHT, span] = re.astype(BF)
            spread[SG + at : SG + at + HEIGHT, span] = im.astype(BF)
            if block + 1 < STEPS:
                re, im = re * step_cos - im * step_sin, re * step_sin + im * step_cos
    both = dot_nt(spread[...], col_t[...])
    weight = aterm[...].astype(F32) * (1.0 / SG)
    g_re = (both[:SG, :SG] - both[SG:, SG:]) * weight
    g_im = (both[:SG, SG:] + both[SG:, :SG]) * weight
    grid = jnp.concatenate([g_re, g_im], 0).astype(BF)
    low = dot_tn(lift[...], grid).astype(BF)
    back = dot_nt(low, k_right[:, :SG])
    for f in range(NF):
        top = back[f * 16 : f * 16 + 8]
        bot = back[f * 16 + 8 : f * 16 + 16]
        re = top[:, :M] - bot[:, M:]
        im = bot[:, :M] + top[:, M:]
        cos = phase[0, f : f + 1, :]
        sin = phase[1, f : f + 1, :]
        both_parts = jnp.concatenate([re * cos + im * sin, im * cos - re * sin], 0).astype(BF)
        for b in range(NB):
            out[f * NB + b] = both_parts


def update_kernel(folded, w_rows, picks, turn, w_high, out, fs, os):
    count = NF * NB
    for s in range(count):
        fs[s * 2 * RD : (s + 1) * 2 * RD, :] = folded[s].astype(F32)
    mask = picks[...]
    columns = []
    for r in range(RD):
        pieces = []
        for part in range(2):
            value = fs[pl.ds(part * RD + r, count, stride=2 * RD), :]
            early = value * mask
            pieces.append(early)
            pieces.append(value - early)
        columns.append(jnp.concatenate(pieces, 0).astype(BF))
    stacked = jnp.concatenate(columns, 1)
    mixed = dot(w_rows[...], stacked)
    t_re = turn[0]
    t_im = turn[1]
    high = w_high[...]
    n_out = NH // NB
    for r in range(RD):
        y_re = mixed[:M, r * M : (r + 1) * M]
        y_im = mixed[M:, r * M : (r + 1) * M]
        z_re = (y_re * t_re - y_im * t_im).astype(BF)
        z_im = (y_re * t_im + y_im * t_re).astype(BF)
        os[pl.ds(r, 2 * n_out, stride=RD), :] = dot_nt(high, jnp.concatenate([z_re, z_im], 1))
    for part in range(2):
        for h in range(n_out):
            at = (part * n_out + h) * RD
            out[part, :, h * M : (h + 1) * M] = os[at : at + RD, :]


def shape(*dims, dtype=BF):
    return jax.ShapeDtypeStruct(dims, dtype)


SMEM = pl.BlockSpec(memory_space=pltpu.SMEM)
VMEM = pl.BlockSpec(memory_space=pltpu.VMEM)
HBM = pl.BlockSpec(memory_space=pltpu.HBM)
ANY = pl.BlockSpec(memory_space=pl.ANY)
PARAMS = pltpu.CompilerParams(vmem_limit_bytes=24 * 2**20)


def buf(*dims, dtype=BF):
    return pltpu.VMEM(dims, dtype)


def smem(*dims):
    return pltpu.SMEM(dims, jnp.int32)


def sems(count):
    return pltpu.SemaphoreType.DMA((count,))


def call(kernel, specs, outs, scratch, name, places=None, cost=None):
    single = not isinstance(outs, (list, tuple))
    return pl.pallas_call(
        kernel,
        out_shape=outs,
        in_specs=specs,
        out_specs=places or (VMEM if single else [VMEM] * len(outs)),
        scratch_shapes=scratch,
        compiler_params=PARAMS,
        cost_estimate=cost,
        name=name,
    )


def partner(value, mask):
    pairs = [(source, source ^ mask) for source in range(NT)]
    return lax.ppermute(value, "team", pairs)


def local(facet_rows, sub_offsets, facet_offsets, aterm, cells, observed, weights, counts):
    t = tables()
    offs = sub_offsets.T
    foffs = facet_offsets.T
    live = counts.transpose(1, 2, 0)
    keep = lambda array: pltpu.with_memory_space_constraint(array, pltpu.HBM)
    offs = keep(offs)
    foffs = keep(foffs)
    ids = [smem(2, NF * NB), smem(2, NF)]
    others = [partner(cells, mask) for mask in NEAR[1:]]
    windows, offs_v, foffs_v, cells_v = call(
        forward_kernel,
        [HBM] * 6,
        [
            shape(NF, 2 * RD, M),
            shape(2, NF * NB, dtype=jnp.int32),
            shape(2, NF, dtype=jnp.int32),
            shape(NB, 2, VB, dtype=jnp.int32),
        ],
        [
            smem(2, NF * NB),
            buf(2, RD, L),
            buf(2 * M, 2 * NH),
            buf(2, M, M, dtype=F32),
            buf(2 * NH * RD, M, dtype=F32),
            buf(NF * 2 * RD, M, dtype=F32),
            sems(7),
        ],
        "windows",
    )(
        offs, foffs, keep(cells), keep(facet_rows),
        keep(t["fwd_rows"]), keep(t["fwd_turn"]),
    )
    *others, windows = lax.optimization_barrier((*others, windows))
    near = jnp.stack([part.reshape(NB, 2, VB) for part in [cells_v] + others])
    far = partner(near, FAR)
    arrived = lax.all_to_all(windows, "facet", 0, 0, tiled=True)
    col_t, row_fac, lift, k_right, own_map, tail, phase, w_rows, picks, turn, w_high = call(
        setup_kernel,
        [VMEM] * 2 + [ANY] * 2 + [HBM] * 7,
        [
            shape(2 * SG, NV),
            shape(24, NV, dtype=F32),
            shape(2 * SG, 2 * M),
            shape(2 * M, 2 * SG),
            shape(SG, SG),
            shape(SENT - OBS, M, dtype=F32),
            shape(2, NF, M, dtype=F32),
            shape(2 * M, 4 * NF * NB),
            shape(NF * NB, M, dtype=F32),
            shape(2, M, M, dtype=F32),
            shape(NH, 2 * M),
        ],
        ids
        + [smem(NB, NT, NF)]
        + [buf(NT // 2, 2, VB, dtype=jnp.int32)] * 2
        + [
            buf(2 * SG, 2 * M),
            buf(NT, 2, VB, dtype=jnp.int32),
            buf(2, VB),
            buf(2, VB),
            sems(11),
        ],
        "setup",
        cost=pl.CostEstimate(flops=20 * 10**9, transcendentals=0, bytes_accessed=2**22),
    )(
        offs_v, foffs_v, near, far, keep(t["k_left"]),
        keep(aterm), keep(observed), keep(weights.transpose(0, 2, 1, 3)),
        keep(live), keep(t["bwd_turn"]), keep(t["bwd_high"]),
    )
    parts = call(
        predict_kernel,
        [VMEM] * 8,
        shape(NT, SENT, M),
        [buf(SENT, M, dtype=F32)],
        "predict",
    )(arrived, lift, k_right, own_map, col_t, row_fac, tail, phase)
    gathered = lax.all_to_all(parts, "team", 0, 0, tiled=True)
    folded = call(
        grid_kernel,
        [VMEM] * 7,
        shape(NF * NB, 2 * RD, M),
        [
            buf(2 * SG, NV),
            buf(OBS, M, dtype=F32),
            buf(NT, SENT - OBS, M, dtype=F32),
        ],
        "grid",
    )(gathered, col_t, row_fac, own_map, lift, k_right, phase)
    returned = lax.all_to_all(folded, ("facet", "sub"), 0, 0, tiled=True)
    update = call(
        update_kernel,
        [VMEM] * 5,
        shape(2, RD, L // NB, dtype=F32),
        [buf(NF * NB * 2 * RD, M, dtype=F32), buf(NH * RD, M, dtype=F32)],
        "update",
    )(returned, w_rows, picks, turn, w_high)
    return update[None]


def solution(mesh):
    placed = (
        P("facet", None, "team", None),
        P(),
        P(),
        P("facet", None, None, None),
        P("facet", None, "team", None, None),
        P("facet", None, "team", None, None),
        P("facet", None, "team", None),
        P(),
    )
    return jax.shard_map(
        local,
        mesh=mesh,
        in_specs=placed,
        out_specs=P("facet", None, "team", "sub"),
        check_vma=False,
    )
```

```python
import math

import jax
import jax.numpy as jnp
import numpy as np
from jax import lax
from jax.experimental import pallas as pl
from jax.experimental.pallas import tpu as pltpu
from jax.sharding import PartitionSpec as P

L = 4096
M = 128
SG = 256
VB = 256
R = 64
NF = 16
NT = 8
NB = 2
RD = R // NT
NH = L // M
NV = NT * VB
TWO_PI = 2.0 * math.pi
FAR = 6
BF = jnp.bfloat16
F32 = jnp.float32

ROOT = np.exp(2j * np.pi * np.arange(L) / L)


def wave(left, right, period, sign):
    steps = (np.outer(left, right) % period) * (L // period)
    table = ROOT[steps]
    return table if sign > 0 else table.conj()


def as_real(matrix):
    return np.block([[matrix.real, -matrix.imag], [matrix.imag, matrix.real]])


def half(matrix):
    return jnp.asarray(np.asarray(matrix, np.float32), BF)


def tables():
    lanes = np.arange(M)
    highs = np.arange(NH)
    fwd_rows = as_real(wave(lanes, highs, NH, -1))
    fwd_turn = wave(lanes, lanes, L, -1)
    bwd_turn = wave(lanes, lanes, L, 1) / math.sqrt(M)
    bwd_full = wave(highs, lanes, NH, 1)
    bwd_high = np.stack([as_real(part) for part in np.split(bwd_full, NB)])
    k_table = wave(lanes, np.arange(SG), SG, 1) / math.sqrt(M)
    k_left = as_real(k_table.T)
    return {
        "fwd_rows": half(fwd_rows),
        "fwd_turn": jnp.asarray(np.stack([fwd_turn.real, fwd_turn.imag]), F32),
        "bwd_turn": jnp.asarray(np.stack([bwd_turn.real, bwd_turn.imag]), F32),
        "bwd_high": half(bwd_high),
        "k_left": half(k_left),
    }


COS_TERMS = [(-1.0) ** n / math.factorial(2 * n) for n in range(9)]
SIN_TERMS = [(-1.0) ** n / math.factorial(2 * n + 1) for n in range(8)]


def turn_angle(steps, period):
    steps = steps & (period - 1)
    steps = jnp.where(steps >= period // 2, steps - period, steps)
    return steps.astype(F32) * (TWO_PI / period)


def series(square, terms):
    total = jnp.full_like(square, terms[-1])
    for term in terms[-2::-1]:
        total = total * square + term
    return total


def cos_of(angle):
    return series(angle * angle, COS_TERMS)


def sin_of(angle):
    return angle * series(angle * angle, SIN_TERMS)


def dot(left, right):
    return jnp.dot(left, right, preferred_element_type=F32)


def dot_tn(left, right):
    return lax.dot_general(left, right, (((0,), (0,)), ((), ())), preferred_element_type=F32)


def dot_nt(left, right):
    return lax.dot_general(left, right, (((1,), (1,)), ((), ())), preferred_element_type=F32)


def fetch(pairs, sems):
    copies = []
    for at, (source, target) in enumerate(pairs):
        copy = pltpu.make_async_copy(source, target, sems.at[at])
        copy.start()
        copies.append(copy)
    return copies


def lead_kernel(out):
    out[...] = jnp.zeros_like(out)


def forward_kernel(
    lead, offs_in, foffs_in, rows, w_rows, turn, out, offs_v, foffs_v, xs, xo
):
    side = lax.axis_index("sub")
    offs_v[...] = offs_in[...]
    foffs_v[...] = foffs_in[...]
    place = lax.broadcasted_iota(jnp.int32, (NF, NF * NB), 1)
    owner = lax.broadcasted_iota(jnp.int32, (NF, NF * NB), 0)
    columns = jnp.broadcast_to(offs_in[1:2, :].astype(F32), (NF, NF * NB))
    tuning = jnp.sum(jnp.where(place == owner * NB + side, columns, 0.0), 1, keepdims=True)
    tuning = jnp.broadcast_to(tuning, (NF, 2 * M)).astype(jnp.int32)
    lane = lax.broadcasted_iota(jnp.int32, (NF, 2 * M), 1)
    pick = lane[:, :M] >= (tuning[:, :M] & (M - 1))
    first = (tuning >> 7) * (lane & (M - 1))
    later = lane & (M - 1)
    blocks = []
    for part in range(2):
        for late in range(2):
            steps = (L // NH) * (first + late * later) + (L // 4) * (part - (lane >> 7))
            blocks.append((cos_of(turn_angle(steps, L)) * (1.0 / 64.0)).astype(BF))
    w_high = jnp.concatenate(blocks, 0)
    for part in range(2):
        whole = rows[0, part].astype(F32)
        for high in range(NH):
            xs[pl.ds((part * NH + high) * RD, RD), :] = whole[:, high * M : (high + 1) * M]
    stacked = jnp.concatenate(
        [xs[pl.ds(r, 2 * NH, stride=RD), :].astype(BF) for r in range(RD)], 1
    )
    mixed = dot(w_rows[...], stacked)
    t_re = turn[0]
    t_im = turn[1]
    for r in range(RD):
        y_re = mixed[:M, r * M : (r + 1) * M]
        y_im = mixed[M:, r * M : (r + 1) * M]
        z_re = (y_re * t_re - y_im * t_im).astype(BF)
        z_im = (y_re * t_im + y_im * t_re).astype(BF)
        found = dot_nt(w_high, jnp.concatenate([z_re, z_im], 1))
        for part in range(2):
            at = part * 2 * NF
            value = jnp.where(pick, found[at : at + NF], found[at + NF : at + 2 * NF])
            xo[pl.ds(part * RD + r, NF, stride=2 * RD), :] = value
    for a in range(NF):
        out[a] = xo[a * 2 * RD : (a + 1) * 2 * RD, :].astype(BF)


SENT = 40
OBS = 2 * NV // M
HEIGHT = 16
STEPS = SG // HEIGHT


def setup_kernel(
    offs_v, foffs_v, near_h, far_h, k_left_h, aterm_h, seen_h, weights_h, counts_h, turn_h, w_high_h,
    col_t, row_fac, lift, k_right, aterm, tail, phase, w_rows, picks, turn, w_high,
    offs, foffs, counts, near, far, k_left, spots, seen, weights, sems,
):
    facet = lax.axis_index("facet")
    team = lax.axis_index("team")
    side = lax.axis_index("sub")
    copies = fetch(
        [
            (offs_v, offs),
            (foffs_v, foffs),
            (k_left_h, k_left),
            (near_h.at[:, side], near),
            (far_h.at[:, side], far),
            (aterm_h.at[0, side], aterm),
            (seen_h.at[0, side, 0], seen),
            (weights_h.at[0, 0], weights),
            (counts_h, counts),
            (turn_h, turn),
            (w_high_h.at[side], w_high),
        ],
        sems,
    )
    for copy in copies[:2]:
        copy.wait()
    shift_u = offs[0, facet * NB + side]
    row = lax.broadcasted_iota(jnp.int32, (2 * RD, 2 * M), 0)
    lane = lax.broadcasted_iota(jnp.int32, (2 * RD, 2 * M), 1)
    p = lane & (M - 1)
    quarter = ((row >> 3) - (lane >> 7)) * (L // 4)
    row_turn = (L // R) * (p + shift_u) * (team * RD + (row & (RD - 1)))
    base = quarter - row_turn
    blocks = []
    for f in range(NF):
        steps = base + p * foffs[0, f]
        blocks.append((cos_of(turn_angle(steps, L)) * (1.0 / 32.0)).astype(BF))
    joined = jnp.concatenate(blocks, 0)
    own = offs[1, facet * NB + side]
    row = lax.broadcasted_iota(jnp.int32, (NF, M), 0)
    lane = lax.broadcasted_iota(jnp.int32, (NF, M), 1)
    column = jnp.zeros((NF, M), jnp.int32)
    for f in range(NF):
        column = jnp.where(row == f, foffs[1, f], column)
    angle = turn_angle(column * ((lane - own) & (M - 1)), L)
    phase[0] = cos_of(angle)
    phase[1] = sin_of(angle)
    row = lax.broadcasted_iota(jnp.int32, (M, SG), 0)
    lane = lax.broadcasted_iota(jnp.int32, (M, SG), 1)
    angle = turn_angle(((row - own) & (M - 1)) * lane, SG)
    k_re = (cos_of(angle) * (1.0 / math.sqrt(M))).astype(BF)
    k_im = (sin_of(angle) * (1.0 / math.sqrt(M))).astype(BF)
    k_right[:M, :SG] = k_re
    k_right[:M, SG:] = k_im
    k_right[M:, :SG] = -k_im
    k_right[M:, SG:] = k_re
    lane = lax.broadcasted_iota(jnp.int32, (8, M), 1)
    row = lax.broadcasted_iota(jnp.int32, (NF * NB, M), 0)
    high = jnp.zeros((8, M), jnp.int32)
    low = jnp.zeros((NF * NB, M), jnp.int32)
    for s in range(NF * NB):
        high = jnp.where((lane & (NF * NB - 1)) == s, offs[1, s] >> 7, high)
        low = jnp.where(row == s, offs[1, s] & (M - 1), low)
    lane_rows = lax.broadcasted_iota(jnp.int32, (NF * NB, M), 1)
    picks[...] = jnp.where(lane_rows >= low, 1.0, 0.0)
    high = high + ((lane >> 5) & 1)
    quarter = (lane >> 6) * (L // 4)
    high = jnp.concatenate([high] * 4, 0)
    quarter = jnp.concatenate([quarter] * 4, 0)
    for block in range(2 * M // 32):
        spot = lax.broadcasted_iota(jnp.int32, (32, M), 0) + block * 32
        steps = (L // NH) * (spot & (M - 1)) * high + quarter - (spot >> 7) * (L // 4)
        w_rows[block * 32 : (block + 1) * 32, :] = cos_of(turn_angle(steps, L)).astype(BF)
    for copy in copies[2:]:
        copy.wait()
    lift[...] = dot_nt(k_left[...], joined).astype(BF)
    pair = weights[...].astype(F32)
    weight = jnp.where(side == 0, pair[0:1], pair[1:2])
    slot = lax.broadcasted_iota(jnp.int32, (1, VB), 1)
    weight = jnp.where(slot < counts[side, team, facet], weight, 0.0)
    both = seen[...].astype(F32)
    tail[...] = jnp.zeros_like(tail)
    for at in range(2):
        half = slice(at * M, (at + 1) * M)
        tail[at : at + 1, :] = both[0:1, half]
        tail[2 + at : 3 + at, :] = both[1:2, half]
        tail[4 + at : 5 + at, :] = weight[:, half]
    for step in range(NT // 2):
        spots[team ^ step] = near[step]
        spots[team ^ FAR ^ step] = far[step]
    count = lax.broadcasted_iota(jnp.int32, (8, M), 0)

    def turns(place, tile):
        half = slice(tile % 2 * M, (tile % 2 + 1) * M)
        spot = jnp.broadcast_to(spots[tile // 2, place : place + 1, half], (8, M))
        angle = turn_angle(spot * count, 4 * SG)
        step = turn_angle(spot * 8, 4 * SG)
        return cos_of(angle), sin_of(angle), cos_of(step), sin_of(step)

    for tile in range(NV // M):
        lanes = slice(tile * M, (tile + 1) * M)
        cos, sin, step_cos, step_sin = turns(0, tile)
        row_fac[0:8, lanes] = cos
        row_fac[8:16, lanes] = sin
        row_fac[16:17, lanes] = step_cos[0:1]
        row_fac[17:18, lanes] = step_sin[0:1]
        cos, sin, step_cos, step_sin = widen(*turns(1, tile))
        for block in range(STEPS):
            at = block * HEIGHT
            col_t[at : at + HEIGHT, lanes] = cos.astype(BF)
            col_t[SG + at : SG + at + HEIGHT, lanes] = sin.astype(BF)
            if block + 1 < STEPS:
                cos, sin = cos * step_cos - sin * step_sin, cos * step_sin + sin * step_cos


def widen(cos, sin, step_cos, step_sin):
    far_cos = cos * step_cos - sin * step_sin
    far_sin = cos * step_sin + sin * step_cos
    twice_cos = step_cos * step_cos - step_sin * step_sin
    twice_sin = 2.0 * step_cos * step_sin
    return (
        jnp.concatenate([cos, far_cos], 0),
        jnp.concatenate([sin, far_sin], 0),
        twice(twice_cos),
        twice(twice_sin),
    )


def row_factors(row_fac, span):
    width = span.stop - span.start
    return widen(
        row_fac[0:8, span],
        row_fac[8:16, span],
        jnp.broadcast_to(row_fac[16:17, span], (8, width)),
        jnp.broadcast_to(row_fac[17:18, span], (8, width)),
    )


def twice(value):
    return jnp.concatenate([value, value], 0)


def predict_kernel(
    spec, lift, k_right, aterm, col_t, row_fac, tail, phase, out, rows_out
):
    parts = []
    for f in range(NF):
        both = spec[f].astype(F32)
        cos = phase[0, f : f + 1, :]
        sin = phase[1, f : f + 1, :]
        parts.append(both[:RD] * cos - both[RD:] * sin)
        parts.append(both[:RD] * sin + both[RD:] * cos)
    turned = dot(lift[...], jnp.concatenate(parts, 0).astype(BF)).astype(BF)
    image = dot(jnp.concatenate([turned[:SG], turned[SG:]], 1), k_right[...])
    weight = aterm[...].astype(F32)
    w_re = image[:, :SG] * weight
    w_im = image[:, SG:] * weight
    left = jnp.concatenate(
        [
            jnp.concatenate([w_re, w_im], 1).astype(BF),
            jnp.concatenate([w_im, -w_re], 1).astype(BF),
        ],
        0,
    )
    for chunk in range(NT):
        span = slice(chunk * VB, (chunk + 1) * VB)
        z = dot(left, col_t[:, span])
        cos, sin, step_cos, step_sin = row_factors(row_fac, span)
        re = z[SG - HEIGHT : SG]
        im = z[2 * SG - HEIGHT :]
        for block in range(STEPS - 2, -1, -1):
            at = block * HEIGHT
            re, im = (
                re * step_cos + im * step_sin + z[at : at + HEIGHT],
                im * step_cos - re * step_sin + z[SG + at : SG + at + HEIGHT],
            )
        re, im = re * cos + im * sin, im * cos - re * sin
        re = jnp.sum(re, 0, keepdims=True) * (1.0 / SG)
        im = jnp.sum(im, 0, keepdims=True) * (1.0 / SG)
        for tile in range(VB // M):
            at = chunk * (VB // M) + tile
            rows_out[at : at + 1, :] = re[:, tile * M : (tile + 1) * M]
            rows_out[NV // M + at : NV // M + at + 1, :] = im[:, tile * M : (tile + 1) * M]
    rows_out[OBS:, :] = tail[...]
    packed = rows_out[...].astype(BF)
    for peer in range(NT):
        out[peer] = packed


def grid_kernel(
    parts, col_t, row_fac, aterm, lift, k_right, phase, out, spread, res, slots
):
    part = parts[0].astype(F32)
    total = part[:OBS]
    slots[0] = part[OBS:]
    for peer in range(1, NT):
        part = parts[peer].astype(F32)
        total = total + part[:OBS]
        slots[peer] = part[OBS:]
    res[...] = total
    for tile in range(NV // M):
        t = tile // 2
        h = tile % 2
        weight = slots[t, 4 + h : 5 + h, :]
        r_re = weight * (slots[t, h : 1 + h, :] - res[tile : tile + 1, :])
        r_im = weight * (slots[t, 2 + h : 3 + h, :] - res[NV // M + tile : NV // M + tile + 1, :])
        span = slice(tile * M, (tile + 1) * M)
        cos, sin, step_cos, step_sin = row_factors(row_fac, span)
        re, im = r_re * cos - r_im * sin, r_re * sin + r_im * cos
        for block in range(STEPS):
            at = block * HEIGHT
            spread[at : at + HEIGHT, span] = re.astype(BF)
            spread[SG + at : SG + at + HEIGHT, span] = im.astype(BF)
            if block + 1 < STEPS:
                re, im = re * step_cos - im * step_sin, re * step_sin + im * step_cos
    both = dot_nt(spread[...], col_t[...])
    weight = aterm[...].astype(F32) * (1.0 / SG)
    g_re = (both[:SG, :SG] - both[SG:, SG:]) * weight
    g_im = (both[:SG, SG:] + both[SG:, :SG]) * weight
    grid = jnp.concatenate([g_re, g_im], 0).astype(BF)
    low = dot_tn(lift[...], grid).astype(BF)
    back = dot_nt(low, k_right[:, :SG])
    for f in range(NF):
        top = back[f * 16 : f * 16 + 8]
        bot = back[f * 16 + 8 : f * 16 + 16]
        re = top[:, :M] - bot[:, M:]
        im = bot[:, :M] + top[:, M:]
        cos = phase[0, f : f + 1, :]
        sin = phase[1, f : f + 1, :]
        both_parts = jnp.concatenate([re * cos + im * sin, im * cos - re * sin], 0).astype(BF)
        for b in range(NB):
            out[f * NB + b] = both_parts


def update_kernel(folded, w_rows, picks, turn, w_high, out, fs, os):
    count = NF * NB
    for s in range(count):
        fs[s * 2 * RD : (s + 1) * 2 * RD, :] = folded[s].astype(F32)
    mask = picks[...]
    columns = []
    for r in range(RD):
        pieces = []
        for part in range(2):
            value = fs[pl.ds(part * RD + r, count, stride=2 * RD), :]
            early = value * mask
            pieces.append(early)
            pieces.append(value - early)
        columns.append(jnp.concatenate(pieces, 0).astype(BF))
    stacked = jnp.concatenate(columns, 1)
    mixed = dot(w_rows[...], stacked)
    t_re = turn[0]
    t_im = turn[1]
    high = w_high[...]
    n_out = NH // NB
    for r in range(RD):
        y_re = mixed[:M, r * M : (r + 1) * M]
        y_im = mixed[M:, r * M : (r + 1) * M]
        z_re = (y_re * t_re - y_im * t_im).astype(BF)
        z_im = (y_re * t_im + y_im * t_re).astype(BF)
        os[pl.ds(r, 2 * n_out, stride=RD), :] = dot_nt(high, jnp.concatenate([z_re, z_im], 1))
    for part in range(2):
        for h in range(n_out):
            at = (part * n_out + h) * RD
            out[part, :, h * M : (h + 1) * M] = os[at : at + RD, :]


def shape(*dims, dtype=BF):
    return jax.ShapeDtypeStruct(dims, dtype)


SMEM = pl.BlockSpec(memory_space=pltpu.SMEM)
VMEM = pl.BlockSpec(memory_space=pltpu.VMEM)
HBM = pl.BlockSpec(memory_space=pltpu.HBM)
ANY = pl.BlockSpec(memory_space=pl.ANY)
PARAMS = pltpu.CompilerParams(vmem_limit_bytes=24 * 2**20)


def buf(*dims, dtype=BF):
    return pltpu.VMEM(dims, dtype)


def smem(*dims):
    return pltpu.SMEM(dims, jnp.int32)


def sems(count):
    return pltpu.SemaphoreType.DMA((count,))


def call(kernel, specs, outs, scratch, name, places=None, cost=None):
    single = not isinstance(outs, (list, tuple))
    return pl.pallas_call(
        kernel,
        out_shape=outs,
        in_specs=specs,
        out_specs=places or (VMEM if single else [VMEM] * len(outs)),
        scratch_shapes=scratch,
        compiler_params=PARAMS,
        cost_estimate=cost,
        name=name,
    )


def partner(value, mask):
    pairs = [(source, source ^ mask) for source in range(NT)]
    return lax.ppermute(value, "team", pairs)


def local(facet_rows, sub_offsets, facet_offsets, aterm, cells, observed, weights, counts):
    t = tables()
    offs = sub_offsets.T
    foffs = facet_offsets.T
    live = counts.transpose(1, 2, 0)
    keep = lambda array: pltpu.with_memory_space_constraint(array, pltpu.HBM)
    ids = [smem(2, NF * NB), smem(2, NF)]
    lead = call(
        lead_kernel,
        [],
        shape(8, M, dtype=F32),
        [],
        "lead",
        cost=pl.CostEstimate(flops=20 * 10**9, transcendentals=0, bytes_accessed=2**12),
    )()
    cells, lead = lax.optimization_barrier((cells, lead))
    others = [partner(cells, mask) for mask in (1, 2, 3)]
    windows, offs_v, foffs_v = call(
        forward_kernel,
        [ANY] + [VMEM] * 5,
        [
            shape(NF, 2 * RD, M),
            shape(2, NF * NB, dtype=jnp.int32),
            shape(2, NF, dtype=jnp.int32),
        ],
        [
            buf(2 * NH * RD, M, dtype=F32),
            buf(NF * 2 * RD, M, dtype=F32),
        ],
        "windows",
    )(
        lead, offs, foffs, facet_rows, t["fwd_rows"], t["fwd_turn"],
    )
    *others, windows = lax.optimization_barrier((*others, windows))
    near = jnp.stack([part.reshape(NB, 2, VB) for part in [cells] + others])
    far = partner(near, FAR)
    arrived = lax.all_to_all(windows, "facet", 0, 0, tiled=True)
    col_t, row_fac, lift, k_right, own_map, tail, phase, w_rows, picks, turn, w_high = call(
        setup_kernel,
        [VMEM] * 2 + [ANY] * 2 + [HBM] * 7,
        [
            shape(2 * SG, NV),
            shape(24, NV, dtype=F32),
            shape(2 * SG, 2 * M),
            shape(2 * M, 2 * SG),
            shape(SG, SG),
            shape(SENT - OBS, M, dtype=F32),
            shape(2, NF, M, dtype=F32),
            shape(2 * M, 4 * NF * NB),
            shape(NF * NB, M, dtype=F32),
            shape(2, M, M, dtype=F32),
            shape(NH, 2 * M),
        ],
        ids
        + [smem(NB, NT, NF)]
        + [buf(NT // 2, 2, VB, dtype=jnp.int32)] * 2
        + [
            buf(2 * SG, 2 * M),
            buf(NT, 2, VB, dtype=jnp.int32),
            buf(2, VB),
            buf(2, VB),
            sems(11),
        ],
        "setup",
        cost=pl.CostEstimate(flops=20 * 10**9, transcendentals=0, bytes_accessed=2**22),
    )(
        offs_v, foffs_v, near, far, keep(t["k_left"]),
        keep(aterm), keep(observed), keep(weights.transpose(0, 2, 1, 3)),
        keep(live), keep(t["bwd_turn"]), keep(t["bwd_high"]),
    )
    parts = call(
        predict_kernel,
        [VMEM] * 8,
        shape(NT, SENT, M),
        [buf(SENT, M, dtype=F32)],
        "predict",
    )(arrived, lift, k_right, own_map, col_t, row_fac, tail, phase)
    gathered = lax.all_to_all(parts, "team", 0, 0, tiled=True)
    folded = call(
        grid_kernel,
        [VMEM] * 7,
        shape(NF * NB, 2 * RD, M),
        [
            buf(2 * SG, NV),
            buf(OBS, M, dtype=F32),
            buf(NT, SENT - OBS, M, dtype=F32),
        ],
        "grid",
    )(gathered, col_t, row_fac, own_map, lift, k_right, phase)
    returned = lax.all_to_all(folded, ("facet", "sub"), 0, 0, tiled=True)
    update = call(
        update_kernel,
        [VMEM] * 5,
        shape(2, RD, L // NB, dtype=F32),
        [buf(NF * NB * 2 * RD, M, dtype=F32), buf(NH * RD, M, dtype=F32)],
        "update",
    )(returned, w_rows, picks, turn, w_high)
    return update[None]


def solution(mesh):
    placed = (
        P("facet", None, "team", None),
        P(),
        P(),
        P("facet", None, None, None),
        P("facet", None, "team", None, None),
        P("facet", None, "team", None, None),
        P("facet", None, "team", None),
        P(),
    )
    return jax.shard_map(
        local,
        mesh=mesh,
        in_specs=placed,
        out_specs=P("facet", None, "team", "sub"),
        check_vma=False,
    )
```
